128 devices in a mesh: wide: 8 (over y, core), narrow: 16 (over z, x).
Axes of the slice: x: 4, y: 4, z: 4, core: 2. Of those that a mesh axis runs over, the one named last changes fastest.
Arguments:
- queries: bfloat16 [32768, 128], P(('wide', 'narrow')), may hold values from -6 to 6
- index_rows: bfloat16 [1048576, 128], P(('wide', 'narrow')), may hold values from -6 to 6
- lse_shift: float32 [32768], P('wide'), may hold values from 0 to 2.5
- loss_weight: float32 [32768], P('wide'), may hold values from 4 to 32
- positives: int32 [32768], P('wide'), may hold values from 0 to 131071
- tile_negs: int32 [256, 512], P('wide'), may hold values from 0 to 1023
- fetch_owner: int32 [8192, 1], P(('wide', 'narrow')), may hold values from 0 to 127; in each aligned block of 64 rows (0 to 63, 64 to 127, ...) at most 2 rows name the same one
- fetch_local: int32 [8192], P(('wide', 'narrow')), may hold values from 0 to 63
Outputs:
- query_grad: float32 [32768, 128], P(('wide', 'narrow'))
- index_grad: float32 [1048576, 128], P(('wide', 'narrow'))
The draws below stay inside these ranges and needn't reach their ends.
Inputs may be any that keep to these rules, and one draw needn't show every extreme that they name: `fetch_owner`: among the 64 fetches of one device no owner is named more than 2 times, a bound that some block reaches.
All inputs are finite; a program needn't handle non-finite values.
Results may differ from the reference program's by a relative error of at most 0.0043.
Values may be sent and summed in bfloat16 or wider, within the bound.
No kernel may reach another device: no remote copies, remote signals or barrier semaphores. Data moves between devices by JAX's collectives and lax.ppermute only.
A program may use at most 128 MiB of HBM per device.

```python
import math
import jax
import jax.numpy as jnp
import numpy as np
from jax import lax

D = 128
BLOCK = 128
QTILE = 128
CAP = 2
NB_DEV = 64
FETCH = 64
Q_GRP = 4096
QUERIES = 32768
SLOTS_GRP = 1024
KT = 512
TILES = 256
INDEX_ROWS = 1048576
N_WIDE = 8
N_NARROW = 16
DEVICES = 128


def with_ends(result, own_key, least, largest):
    longest = result.shape.index(max(result.shape))
    spots = []
    for shift in (0, 1):
        where = [jax.random.randint(jax.random.fold_in(own_key, axis), (), 0, length) for axis, length in enumerate(result.shape)]
        where[longest] = (where[longest] + shift) % result.shape[longest]
        spots.append(tuple(where))
    return result.at[spots[0]].set(least).at[spots[1]].set(largest)


def levels(rng, dims, shards, least, top_value):
    gain = 1.0
    for dim, blocks in shards:
        steps = jax.random.uniform(jax.random.fold_in(jax.random.fold_in(rng, 6), dim), (blocks,), jnp.float32, least / len(shards), top_value / len(shards))
        gain = gain * jnp.repeat(jnp.exp(steps), dims[dim] // blocks).reshape((-1,) + (1,) * (len(dims) - 1 - dim))
    return gain


def assign_block(key, own, number, rows, count, top, limit, lean):
    sequence = jax.random.permutation(key, count)
    packed, usual = shares(count, rows * top, limit, lean, True), shares(count, rows * top, limit, lean, False)
    places = jnp.arange(count)

    def named(lengths, turn):
        used = int((lengths > 0).sum())
        fixed = max(1, used // 4)
        moved = fixed + (places - fixed + turn * (used - fixed)) % max(1, count - fixed)
        return jnp.zeros((count,), jnp.int32).at[sequence[jnp.where(places < fixed, places, moved)]].set(jnp.asarray(lengths, jnp.int32))

    lengths = jnp.where(number % 4 == 0, named(packed, number // 4), named(usual, number - number // 4 - 1))
    mixed = jax.random.permutation(jax.random.fold_in(own, 3), count)
    donor, sink = mixed[0:count // 2 * 2:2], mixed[1:count // 2 * 2:2]
    room = jnp.minimum(lengths[donor] - 1, limit - lengths[sink]) // 2
    room = jnp.where((donor == sequence[0]) | (sink == sequence[0]) | (lengths[sink] == 0), 0, jnp.maximum(room, 0))
    moved = jax.random.randint(jax.random.fold_in(own, 4), (count // 2,), 0, 1 << 20) % (room + 1)
    lengths = lengths.at[donor].add(-moved).at[sink].add(moved)
    labels = jnp.searchsorted(jnp.cumsum(lengths), jnp.arange(rows * top), side="right").astype(jnp.int32)
    grid = labels.reshape(top, rows).T
    grid = grid[jax.random.permutation(jax.random.fold_in(own, 1), rows)]
    turn = jax.random.randint(jax.random.fold_in(own, 2), (rows, 1), 0, top)
    return jnp.take_along_axis(grid, (jnp.arange(top)[None, :] + turn) % top, axis=1)


def shares(count, total, limit, skew, full):
    loads = [(1 << 20) // math.isqrt(rank ** skew) + 1 for rank in range(1, count + 1)]
    largest = limit if full else min(limit, max(-(-total // count), total * loads[0] // sum(loads)))
    least = 1 if total - largest >= count - 1 else 0
    counts, surplus = [largest] + [least] * (count - 1), total - largest - least * (count - 1)
    while surplus > 0:
        free = [i for i in range(1, count) if counts[i] < largest] or [i for i in range(1, count) if counts[i] < limit]
        whole, remaining = sum([loads[i] for i in free]), surplus
        for i in free:
            more = min(limit - counts[i], max(1, remaining * loads[i] // whole), surplus)
            counts[i] = counts[i] + more
            surplus = surplus - more
    return np.array(counts)


def bell_draw(rng, extent, scale, reach, shards=(), kind=jnp.bfloat16):
    factor_of = levels(rng, extent, shards, -0.22, 0.18) if shards else 1.0
    entries = jax.random.normal(rng, extent, jnp.float32) * scale * factor_of
    return jnp.minimum(jnp.maximum(entries, -reach), reach).astype(kind)


def setup_inputs(seed: int = 0) -> dict:
    seeds = jax.random.split(jax.random.key(seed), 9)
    queries = bell_draw(seeds[0], (QUERIES, D), 1.0, 6.0, ((0, 128),))
    index_rows = bell_draw(seeds[1], (INDEX_ROWS, D), 1.0, 6.0, ((0, 128),))
    lse_shift = jnp.clip(2.5 * jax.random.uniform(seeds[2], (QUERIES,), jnp.float32) ** levels(seeds[2], (QUERIES,), ((0, 8),), -0.2, 0.2), 0.0, 2.5)
    loss_weight = jnp.clip(jnp.exp(math.log(32.0) - 2.0794415 * jax.random.uniform(seeds[3], (QUERIES,), jnp.float32) ** levels(seeds[3], (QUERIES,), ((0, 8),), -0.2, 0.2)), 4.0, 32.0)
    positives = with_ends(jax.random.randint(seeds[4], (QUERIES,), 0, SLOTS_GRP * BLOCK), jax.random.fold_in(seeds[4], 1), 0, (SLOTS_GRP * BLOCK) - 1).astype(jnp.int32)
    tile_negs = with_ends(jax.random.randint(seeds[5], (TILES, KT), 0, SLOTS_GRP), jax.random.fold_in(seeds[5], 1), 0, SLOTS_GRP - 1).astype(jnp.int32)
    fetch_owner_keys = jax.random.split(jax.random.fold_in(seeds[6], 1), (DEVICES * FETCH) // FETCH)
    fetch_owner_turns = jax.random.permutation(jax.random.fold_in(seeds[6], 3), (DEVICES * FETCH) // FETCH)
    fetch_owner = jax.vmap(lambda own, number: assign_block(jax.random.fold_in(seeds[6], 2), own, number, FETCH, DEVICES, 1, CAP, 2))(fetch_owner_keys, fetch_owner_turns).reshape((DEVICES * FETCH, 1))
    fetch_local = with_ends(jax.random.randint(seeds[7], (DEVICES * FETCH,), 0, NB_DEV), jax.random.fold_in(seeds[7], 1), 0, NB_DEV - 1).astype(jnp.int32)
    return dict(queries=queries, index_rows=index_rows, lse_shift=lse_shift, loss_weight=loss_weight, positives=positives, tile_negs=tile_negs, fetch_owner=fetch_owner, fetch_local=fetch_local)


def device_terms(group_queries, lse_full, loss_rows, pos_rows, negs_rows, fetched, narrow_pos):
    score_scale = 2.0 / math.sqrt(D)
    column_count = FETCH * BLOCK
    scores = jnp.dot(group_queries, fetched.T, preferred_element_type=jnp.float32) * score_scale
    slot_ids = narrow_pos * FETCH + jnp.arange(FETCH, dtype=jnp.int32)
    tile_hit = jnp.any(negs_rows[:, :, None] == slot_ids[None, None, :], axis=1)
    query_hit = jnp.repeat(tile_hit, QTILE, axis=0)
    pos_hit = (pos_rows // BLOCK)[:, None] == slot_ids[None, :]
    weight = jnp.logical_or(query_hit, pos_hit).astype(jnp.float32)
    weight = jnp.repeat(weight, BLOCK, axis=1)
    column_ids = narrow_pos * column_count + jnp.arange(column_count, dtype=jnp.int32)
    target = (pos_rows[:, None] == column_ids[None, :]).astype(jnp.float32)
    softmax_terms = jnp.exp(scores - lse_full[:, None])
    logit_grad = (loss_rows[:, None] * (weight * softmax_terms - target)).astype(jnp.bfloat16)
    query_part = jnp.dot(logit_grad, fetched, preferred_element_type=jnp.float32) * score_scale
    block_part = (jnp.dot(logit_grad.T, group_queries, preferred_element_type=jnp.float32) * score_scale).astype(jnp.bfloat16)
    return (query_part, block_part)

def reference(queries, index_rows, lse_shift, loss_weight, positives, tile_negs, fetch_owner, fetch_local):
    device_total = N_WIDE * N_NARROW
    index_blocks = index_rows.reshape(device_total * NB_DEV, BLOCK, D)
    lse_all = lse_shift + math.log(SLOTS_GRP * BLOCK)
    tile_count = Q_GRP // QTILE

    def one_device(totals, device):
        query_grad, index_grad = totals
        group_idx = device // N_NARROW
        narrow_pos = device % N_NARROW
        first = group_idx * Q_GRP
        group_queries = lax.dynamic_slice_in_dim(queries, first, Q_GRP, 0)
        lse_rows = lax.dynamic_slice_in_dim(lse_all, first, Q_GRP, 0)
        loss_rows = lax.dynamic_slice_in_dim(loss_weight, first, Q_GRP, 0)
        pos_rows = lax.dynamic_slice_in_dim(positives, first, Q_GRP, 0)
        negs_rows = lax.dynamic_slice_in_dim(tile_negs, group_idx * tile_count, tile_count, 0)
        owners = lax.dynamic_slice_in_dim(fetch_owner[:, 0], device * FETCH, FETCH, 0)
        local_ids = lax.dynamic_slice_in_dim(fetch_local, device * FETCH, FETCH, 0)
        block_ids = (owners * NB_DEV + local_ids).astype(jnp.int32)
        fetched = jnp.take(index_blocks, block_ids, axis=0).reshape(FETCH * BLOCK, D)
        query_part, block_part = device_terms(group_queries, lse_rows, loss_rows, pos_rows, negs_rows, fetched, narrow_pos)
        current = lax.dynamic_slice_in_dim(query_grad, first, Q_GRP, 0)
        query_grad = lax.dynamic_update_slice_in_dim(query_grad, current + query_part, first, 0)
        index_grad = index_grad.at[block_ids].add(block_part.reshape(FETCH, BLOCK, D).astype(jnp.float32))
        return ((query_grad, index_grad), None)
    zeros_init = (jnp.zeros((QUERIES, D), jnp.float32), jnp.zeros((device_total * NB_DEV, BLOCK, D), jnp.float32))
    (query_grad, index_grad), unused = lax.scan(one_device, zeros_init, jnp.arange(device_total, dtype=jnp.int32))
    return (query_grad, index_grad.reshape(INDEX_ROWS, D))
```

```python
import functools
import math

import jax
import jax.numpy as jnp
from jax import lax
from jax.experimental import pallas as pl
from jax.experimental.pallas import tpu as pltpu
from jax.sharding import Mesh
from jax.sharding import PartitionSpec as P

BLOCK = 128
QTILE = 128
CAP = 2
SAME_CORE = ("y", "z", "x")
NARROW = ("z", "x")
PLACES = 2 * CAP
FIELDS = 8
DEAD = -1e30
VMEM_LIMIT = 60 * 1024 * 1024


def bits_low_high(flags):
    half = flags.shape[0] // 2
    powers = jnp.left_shift(1, jnp.arange(half, dtype=jnp.int32)).astype(jnp.float32)[:, None]
    ones = flags.astype(jnp.float32)
    return jnp.sum(ones[:half] * powers, axis=0), jnp.sum(ones[half:] * powers, axis=0)


def prep_kernel(sources, table, own, mate, turned, items, counts, live, base, hits):
    per_source = PLACES * FIELDS

    def flip(i, carry):
        turned[i] = own[i].T
        turned[i + own.shape[0]] = mate[i].T
        return carry

    lax.fori_loop(0, own.shape[0], flip, 0)

    groups = 4
    in_group = sources // groups
    tile_bits = 7
    dead_tile = sources
    dead = jnp.int32(dead_tile)

    def group_entries(group, cursor):
        def source_entries(n, count):
            src = group * in_group + n
            for place in range(PLACES):
                at = place * FIELDS
                block = table[src, at]
                slot = table[src, at + 1]
                hit = table[src, at + 2] | (table[src, at + 3] << 16)
                some = table[src, at + 4] | (table[src, at + 5] << 16)
                base[count] = ((block - 1) << tile_bits) | (slot << 15)
                live[count] = hit | some
                hits[count] = hit
                count = count + jnp.where(block > 0, 1, 0)
            return count

        entries = lax.fori_loop(0, in_group, source_entries, jnp.int32(0))

        def entry_items(e, cursor):
            first, second = cursor
            start = base[e] + group * in_group
            alive = live[e]
            hit = hits[e]
            empty = base[e] + dead
            out = []
            for h, at in enumerate((first, second)):
                for n in range(in_group):
                    bit = 2 * n + h
                    word = start + n + (((hit >> bit) & 1) << 25)
                    items[h, at] = word
                    at = at + ((alive >> bit) & 1)
                items[h, at] = empty
                out.append(at + (at & 1))
            return tuple(out)

        return lax.fori_loop(0, entries, entry_items, cursor)

    ends = lax.fori_loop(0, groups, group_entries, (jnp.int32(0), jnp.int32(0)))
    for h in range(2):
        for i in range(4):
            items[h, ends[h] + i] = dead
        counts[h] = ends[h] // 2


def chunk_kernel(h, first, last, items, counts, rows, q, blocks, turned, *rest):
    if first:
        (query_out, block_out, q_turned, query_acc, scores, grads) = rest
        block_acc = block_out
    else:
        (block_in, query_out, own_out, mate_out, q_turned, query_acc, scores, grads, block_acc, sem) = rest
        earlier = pltpu.make_async_copy(block_in, block_acc, sem)
        earlier.start()
    scale = 2.0 / math.sqrt(q.shape[2])
    factor = scale * math.log2(math.e)
    tiles = q.shape[0] - 1

    def turn(t, carry):
        q_turned[t] = q[t].T
        query_acc[t] = jnp.zeros((BLOCK, QTILE), jnp.float32)
        return carry

    lax.fori_loop(0, tiles + 1, turn, 0)
    scores[...] = jnp.zeros_like(scores)
    grads[...] = jnp.zeros_like(grads)
    if first:

        def clear(b, carry):
            block_acc[b] = jnp.zeros((BLOCK, QTILE), jnp.float32)
            return carry

        lax.fori_loop(0, block_acc.shape[0], clear, 0)
    else:
        earlier.wait()

    column = lax.broadcasted_iota(jnp.int32, (BLOCK, QTILE), 0)

    def tile_of(word):
        return word & 127

    def block_of(word):
        return (word >> 7) & 127

    def step(i, carry):
        b1, b2, c1, c2 = carry
        a1 = items[h, 2 * i]
        a2 = items[h, 2 * i + 1]
        block = block_of(c1)
        t1, t2 = tile_of(c1), tile_of(c2)
        grad = grads[...]
        both = jnp.concatenate([q[t1], q[t2]], axis=0)
        block_acc[block] += jnp.dot(grad, both, preferred_element_type=jnp.float32)
        part = jnp.dot(turned[block], grad, preferred_element_type=jnp.float32)
        sum1 = query_acc[t1] + part[:, :QTILE]
        sum2 = query_acc[t2] + part[:, QTILE:]
        query_acc[t1] = sum1
        query_acc[t2] = sum2
        slot = (b1 >> 15) & 1023
        for side, word in enumerate((b1, b2)):
            tile = tile_of(word)
            hit = (word >> 25) & 1
            shift = rows[tile, pl.ds(h, 1), :]
            loss = rows[tile, pl.ds(2 + h, 1), :]
            positive = rows[tile, pl.ds(4 + h, 1), :].astype(jnp.int32)
            mine = (positive >> 7) == slot
            shift = jnp.where(jnp.logical_or(mine, hit > 0), shift, DEAD)
            target = jnp.where(mine, positive & 127, -1)
            at = slice(side * QTILE, (side + 1) * QTILE)
            terms = jnp.exp2(scores[:, at] * factor + shift)
            terms = terms - jnp.where(column == target, loss, 0.0)
            grads[:, at] = terms.astype(jnp.bfloat16)
        block = block_of(a1)
        wide = jnp.concatenate([q_turned[tile_of(a1)], q_turned[tile_of(a2)]], axis=1)
        scores[...] = jnp.dot(blocks[block], wide, preferred_element_type=jnp.float32)
        return a1, a2, b1, b2

    dead = jnp.int32(tiles)
    lax.fori_loop(0, counts[h] + 2, step, (dead, dead, dead, dead))

    def finish(t, carry):
        query_out[t] = (query_acc[t] * scale).T.astype(jnp.bfloat16)
        return carry

    lax.fori_loop(0, tiles, finish, 0)
    if last:
        half = own_out.shape[0]

        def deliver(b, carry):
            own_out[b] = block_acc[b] * scale
            mate_out[b] = (block_acc[b + half] * scale).astype(jnp.bfloat16)
            return carry

        lax.fori_loop(0, half, deliver, 0)


def shards(
    queries, index_rows, lse_shift, loss_weight, positives, tile_negs, fetch_owner, fetch_local
):
    narrow_count = lax.axis_size(NARROW)
    sources = lax.axis_size(SAME_CORE)
    core = lax.axis_index("c")
    narrow_pos = lax.axis_index(NARROW)
    feat_width = queries.shape[1]
    own_rows = queries.shape[0]
    blocks_here = index_rows.shape[0] // BLOCK
    stored = index_rows.reshape(blocks_here, BLOCK, feat_width)
    mate_stored = lax.ppermute(stored, "c", [(0, 1), (1, 0)])

    owners = fetch_owner[:, 0]
    fetch_count = owners.shape[0]
    position = jnp.arange(fetch_count, dtype=jnp.int32)
    same_owner = (owners[:, None] == owners[None, :]) & (position[None, :] < position[:, None])
    before = jnp.sum(same_owner.astype(jnp.int32), axis=1)
    owner_wide = owners // narrow_count
    away = (owner_wide % 2) ^ core
    dest = (owner_wide // 2) * narrow_count + owners % narrow_count
    place = away * CAP + before

    slot_ids = narrow_pos * fetch_count + position
    tile_hit = jnp.any(tile_negs[:, :, None] == slot_ids[None, None, :], axis=1)
    tiles = tile_negs.shape[0]
    pos_slots = positives.reshape(tiles, QTILE) // BLOCK
    pos_hit = jnp.any(pos_slots[:, :, None] == slot_ids[None, None, :], axis=1)
    hit_low, hit_high = bits_low_high(tile_hit)
    pos_low, pos_high = bits_low_high(pos_hit)
    as_float = lambda v: v.astype(jnp.float32)
    fields = jnp.stack(
        [
            as_float(away * blocks_here + fetch_local + 1),
            as_float(slot_ids),
            hit_low,
            hit_high,
            pos_low,
            pos_high,
            jnp.zeros((fetch_count,), jnp.float32),
            jnp.zeros((fetch_count,), jnp.float32),
        ],
        axis=0,
    )
    chosen = (dest[None, :] == jnp.arange(sources, dtype=jnp.int32)[:, None])[:, None, :] & (
        place[None, :] == jnp.arange(PLACES, dtype=jnp.int32)[:, None]
    )[None, :, :]
    table = jnp.sum(
        jnp.where(chosen[:, :, None, :], fields[None, None, :, :], 0.0), axis=-1
    ).reshape(sources, PLACES * FIELDS)

    first_row = narrow_pos * own_rows
    lse_own = lax.dynamic_slice_in_dim(lse_shift, first_row, own_rows, 0)
    loss_own = lax.dynamic_slice_in_dim(loss_weight, first_row, own_rows, 0)
    pos_own = lax.dynamic_slice_in_dim(positives, first_row, own_rows, 0)
    lse_full = lse_own + math.log(fetch_count * narrow_count * BLOCK)
    shift = jnp.log2(loss_own) - lse_full * math.log2(math.e)
    per_query = jnp.concatenate([shift, loss_own, as_float(pos_own)]).reshape(6, QTILE)
    per_query = jnp.broadcast_to(per_query[None], (sources, 6, QTILE))
    table_rows = jnp.pad(table, ((0, 0), (0, QTILE - PLACES * FIELDS)))[:, None, :]
    side = jnp.concatenate([per_query, table_rows, jnp.zeros_like(table_rows)], axis=1)
    side = lax.all_to_all(side, SAME_CORE, 0, 0, tiled=True)
    table_in = side[:, 6, : PLACES * FIELDS].astype(jnp.int32)
    dead_rows = jnp.full((1, 8, QTILE), -1.0, jnp.float32)
    rows = jnp.concatenate([side, dead_rows], axis=0)

    halves = []
    for h in range(2):
        part = queries[h * QTILE : (h + 1) * QTILE]
        spread = jnp.broadcast_to(part[None], (sources, QTILE, feat_width))
        part = lax.all_to_all(spread, SAME_CORE, 0, 0, tiled=True)
        halves.append(jnp.concatenate([part, jnp.zeros((1, QTILE, feat_width), part.dtype)]))

    most = sources * PLACES * (tiles // 2) + 32
    smem = pl.BlockSpec(memory_space=pltpu.SMEM)
    vmem = pl.BlockSpec(memory_space=pltpu.VMEM)
    groups = 4
    entries = sources // groups * PLACES + 8
    turned, items, counts = pl.pallas_call(
        functools.partial(prep_kernel, sources),
        out_shape=(
            jax.ShapeDtypeStruct((2 * blocks_here, feat_width, BLOCK), jnp.bfloat16),
            jax.ShapeDtypeStruct((2, most), jnp.int32),
            jax.ShapeDtypeStruct((2,), jnp.int32),
        ),
        in_specs=[smem, vmem, vmem],
        out_specs=(vmem, smem, smem),
        scratch_shapes=[pltpu.SMEM((entries,), jnp.int32)] * 3,
        compiler_params=pltpu.CompilerParams(vmem_limit_bytes=VMEM_LIMIT),
        cost_estimate=pl.CostEstimate(flops=10**9, bytes_accessed=2**24, transcendentals=0),
        name="prep",
    )(table_in, stored, mate_stored)
    blocks = jnp.concatenate([stored, mate_stored])

    acc_shape = jax.ShapeDtypeStruct((2 * blocks_here, BLOCK, feat_width), jnp.float32)
    grad_shape = jax.ShapeDtypeStruct((sources, QTILE, feat_width), jnp.bfloat16)
    own_shape = jax.ShapeDtypeStruct((blocks_here, BLOCK, feat_width), jnp.float32)
    mate_shape = jax.ShapeDtypeStruct((blocks_here, BLOCK, feat_width), jnp.bfloat16)
    scratch = [
        pltpu.VMEM((sources + 1, feat_width, QTILE), jnp.bfloat16),
        pltpu.VMEM((sources + 1, feat_width, QTILE), jnp.float32),
        pltpu.VMEM((BLOCK, 2 * QTILE), jnp.float32),
        pltpu.VMEM((BLOCK, 2 * QTILE), jnp.bfloat16),
    ]
    cost = pl.CostEstimate(flops=2 * 10**10, bytes_accessed=2**25, transcendentals=10**7)
    params = pltpu.CompilerParams(vmem_limit_bytes=VMEM_LIMIT)
    grad_0, acc = pl.pallas_call(
        functools.partial(chunk_kernel, 0, True, False),
        out_shape=(grad_shape, acc_shape),
        in_specs=[smem, smem, vmem, vmem, vmem, vmem],
        out_specs=(vmem, vmem),
        scratch_shapes=scratch,
        compiler_params=params,
        cost_estimate=cost,
        name="chunk_0",
    )(items, counts, rows, halves[0], blocks, turned)
    grad_1, own_grad, mate_grad = pl.pallas_call(
        functools.partial(chunk_kernel, 1, False, True),
        out_shape=(grad_shape, own_shape, mate_shape),
        in_specs=[smem, smem, vmem, vmem, vmem, vmem, pl.BlockSpec(memory_space=pl.ANY)],
        out_specs=(vmem, vmem, vmem),
        scratch_shapes=scratch + [pltpu.VMEM(acc_shape.shape, jnp.float32), pltpu.SemaphoreType.DMA],
        compiler_params=params,
        cost_estimate=cost,
        name="chunk_1",
    )(items, counts, rows, halves[1], blocks, turned, acc)
    sums = []
    for part in (grad_0, grad_1):
        came = lax.all_to_all(part, SAME_CORE, 0, 0, tiled=True)
        sums.append(jnp.sum(came.astype(jnp.float32), axis=0))
    query_grad = jnp.concatenate(sums)
    from_mate = lax.ppermute(mate_grad, "c", [(0, 1), (1, 0)])
    index_grad = (own_grad + from_mate.astype(jnp.float32)).reshape(blocks_here * BLOCK, feat_width)
    return (query_grad, index_grad)


def solution(mesh):
    wide, narrow = mesh.devices.shape
    split = Mesh(mesh.devices.reshape(wide // 2, 2, 4, narrow // 4), ("y", "c", "z", "x"))
    every = ("y", "c", "z", "x")
    group = ("y", "c")
    in_specs = (
        P(every, None),
        P(every, None),
        P(group),
        P(group),
        P(group),
        P(group, None),
        P(every, None),
        P(every),
    )
    out_specs = (P(every, None), P(every, None))
    return jax.shard_map(shards, mesh=split, in_specs=in_specs, out_specs=out_specs, check_vma=False)
```

```python
import functools
import math

import jax
import jax.numpy as jnp
from jax import lax
from jax.experimental import pallas as pl
from jax.experimental.pallas import tpu as pltpu
from jax.sharding import Mesh
from jax.sharding import PartitionSpec as P


BLOCK = 128
QTILE = 128
CAP = 2
SAME_CORE = ("y", "z", "x")
NARROW = ("z", "x")
KEPT = 16
SLAB = 8
STEPS = (("x", 1), ("x", -1), ("y", 1), ("y", -1), ("z", 1), ("z", -1))
PLACES = 2 * CAP * (1 + len(STEPS))
FIELDS = 4
COUNT_AT = PLACES * FIELDS
DEAD = -1e30
UNROLL = 8
VMEM_LIMIT = 60 * 1024 * 1024


def tile_bits(flags):
    places = jnp.arange(flags.shape[0], dtype=jnp.int32)[:, None]
    return jnp.sum(jnp.left_shift(flags.astype(jnp.int32), places), axis=0)


def ask_kernel(sizes, where, owner, local, hits, lives, table):
    ring, narrow_count, blocks_here = sizes
    first_slot, core = where[0], where[1]

    def clear(d, carry):
        table[d, COUNT_AT] = 0
        return carry

    lax.fori_loop(0, table.shape[0], clear, 0)

    def ask(j, carry):
        own, block = owner[j], local[j]
        wide = own // narrow_count
        narrow = own % narrow_count
        turn = jnp.where(block < KEPT, -1, (block - KEPT) // SLAB)
        spot = {"y": wide // 2, "z": narrow // ring, "x": narrow % ring}
        for k, (axis, shift) in enumerate(STEPS):
            spot[axis] = spot[axis] + jnp.where(turn == k, shift + ring, 0)
        dest = ((spot["y"] % ring) * ring + spot["z"] % ring) * ring + spot["x"] % ring
        place = table[dest, COUNT_AT]
        table[dest, COUNT_AT] = place + 1
        at = place * FIELDS
        table[dest, at] = jnp.where(wide % 2 == core, 0, blocks_here) + block
        table[dest, at + 1] = first_slot + j
        table[dest, at + 2] = hits[j]
        table[dest, at + 3] = lives[j]
        return carry

    lax.fori_loop(0, owner.shape[0], ask, 0)


def turn_kernel(own, mate, blocks, turned):
    here = own.shape[0]

    def flip(i, carry):
        blocks[i] = own[i]
        blocks[i + here] = mate[i]
        turned[i] = own[i].T
        turned[i + here] = mate[i].T
        return carry

    lax.fori_loop(0, here, flip, 0)


def list_kernel(table, first_items, second_items, counts, live, base, hits):
    groups = 4
    sources = table.shape[0]
    in_group = sources // groups
    dead = jnp.int32(sources)
    lists = (first_items, second_items)

    def group_entries(group, cursor):
        def source_entries(n, count):
            src = group * in_group + n

            def place_entry(place, count):
                at = place * FIELDS
                base[count] = (table[src, at] << 7) | (table[src, at + 1] << 15)
                hits[count] = table[src, at + 2]
                live[count] = table[src, at + 3]
                return count + 1

            return lax.fori_loop(0, table[src, COUNT_AT], place_entry, count)

        entries = lax.fori_loop(0, in_group, source_entries, jnp.int32(0))

        def entry_items(e, cursor):
            start = base[e] + group * in_group
            alive = live[e]
            hit = hits[e]
            empty = base[e] + dead
            out = []
            for h, at in enumerate(cursor):
                for n in range(in_group):
                    bit = 2 * n + h
                    named = (hit << (25 - bit)) if bit <= 25 else (hit >> (bit - 25))
                    lists[h][at] = (start + n) | (named & (1 << 25))
                    at = at + ((alive >> bit) & 1)
                lists[h][at] = empty
                out.append(at + (at & 1))
            return tuple(out)

        return lax.fori_loop(0, entries, entry_items, cursor)

    ends = lax.fori_loop(0, groups, group_entries, (jnp.int32(0), jnp.int32(0)))
    for h in range(2):
        for i in range(4 * UNROLL):
            lists[h][ends[h] + i] = dead
        counts[h] = (ends[h] + 2 * UNROLL - 1) // (2 * UNROLL)


def chunk_kernel(h, first, last, items, counts, rows, q, blocks, turned, *rest):
    if first:
        (query_out, block_out, q_turned, query_acc, scores, grads) = rest
        block_acc = block_out
    else:
        (block_in, query_out, own_out, mate_out, q_turned, query_acc, scores, grads, block_acc, sem) = rest
        earlier = pltpu.make_async_copy(block_in, block_acc, sem)
        earlier.start()
    scale = 2.0 / math.sqrt(q.shape[2])
    factor = scale * math.log2(math.e)
    tiles = q.shape[0] - 1

    def turn(t, carry):
        q_turned[t] = q[t].T
        query_acc[t] = jnp.zeros((BLOCK, QTILE), jnp.float32)
        return carry

    lax.fori_loop(0, tiles + 1, turn, 0)
    scores[...] = jnp.zeros_like(scores)
    grads[...] = jnp.zeros_like(grads)
    if first:

        def clear(b, carry):
            block_acc[b] = jnp.zeros((BLOCK, QTILE), jnp.float32)
            return carry

        lax.fori_loop(0, block_acc.shape[0], clear, 0)
    else:
        earlier.wait()

    column = lax.broadcasted_iota(jnp.int32, (BLOCK, QTILE), 0)

    def tile_of(word):
        return word & 127

    def block_of(word):
        return (word >> 7) & 127

    def block_grads(words, grad):
        block = block_of(words[0])
        t1, t2 = tile_of(words[0]), tile_of(words[1])
        both = jnp.concatenate([q[t1], q[t2]], axis=0)
        to_block = jnp.dot(grad, both, preferred_element_type=jnp.float32)
        part = jnp.dot(turned[block], grad, preferred_element_type=jnp.float32)
        block_acc[block] += to_block
        sum1 = query_acc[t1] + part[:, :QTILE]
        sum2 = query_acc[t2] + part[:, QTILE:]
        query_acc[t1] = sum1
        query_acc[t2] = sum2

    def logit_grads(words, scores):
        slot = (words[0] >> 15) & 1023
        halves = []
        for side, word in enumerate(words):
            tile = tile_of(word)
            hit = (word >> 25) & 1
            shift = rows[tile, pl.ds(h, 1), :]
            loss = rows[tile, pl.ds(2 + h, 1), :]
            positive = rows[tile, pl.ds(4 + h, 1), :].astype(jnp.int32)
            mine = (positive >> 7) == slot
            shift = jnp.where(jnp.logical_or(mine, hit > 0), shift, DEAD)
            target = jnp.where(mine, positive & 127, -1)
            at = slice(side * QTILE, (side + 1) * QTILE)
            terms = jnp.exp2(scores[:, at] * factor + shift)
            terms = terms - jnp.where(column == target, loss, 0.0)
            halves.append(terms.astype(jnp.bfloat16))
        return jnp.concatenate(halves, axis=1)

    def next_scores(words):
        wide = jnp.concatenate([q_turned[tile_of(words[0])], q_turned[tile_of(words[1])]], axis=1)
        return jnp.dot(blocks[block_of(words[0])], wide, preferred_element_type=jnp.float32)

    def step(i, coming):
        starting = tuple((items[2 * (UNROLL * i + u)], items[2 * (UNROLL * i + u) + 1]) for u in range(UNROLL))
        for u in range(UNROLL):
            grad = logit_grads(coming[u], scores[u])
            block_grads(coming[u], grad)
            scores[u] = next_scores(starting[u])
        return starting

    dead = jnp.int32(tiles)
    lax.fori_loop(0, counts[h] + 1, step, ((dead, dead),) * UNROLL)

    def finish(t, carry):
        query_out[t] = (query_acc[t] * scale).T.astype(jnp.bfloat16)
        return carry

    lax.fori_loop(0, tiles, finish, 0)
    if last:
        half = own_out.shape[0]

        def deliver(b, carry):
            own_out[b] = block_acc[b] * scale
            mate_out[b] = (block_acc[b + half] * scale).astype(jnp.bfloat16)
            return carry

        lax.fori_loop(0, half, deliver, 0)


def shard_work(
    queries, index_rows, lse_shift, loss_weight, positives, tile_negs, fetch_owner, fetch_local
):
    narrow_count = lax.axis_size(NARROW)
    sources = lax.axis_size(SAME_CORE)
    core = lax.axis_index("c")
    narrow_pos = lax.axis_index(NARROW)
    feat_width = queries.shape[1]
    own_rows = queries.shape[0]
    blocks_here = index_rows.shape[0] // BLOCK
    stored = index_rows.reshape(blocks_here, BLOCK, feat_width)
    ring = lax.axis_size("x")
    ways = []
    for axis, shift in STEPS:
        size = lax.axis_size(axis)
        ways.append((axis, [(i, (i + shift) % size) for i in range(size)]))
    slabs = [slice(KEPT + SLAB * k, KEPT + SLAB * (k + 1)) for k in range(len(STEPS))]
    lent = [lax.ppermute(stored[at], axis, way) for at, (axis, way) in zip(slabs, ways)]
    held = jnp.concatenate([stored[:KEPT]] + lent)
    mate_held = lax.ppermute(held, "c", [(0, 1), (1, 0)])

    smem = pl.BlockSpec(memory_space=pltpu.SMEM)
    vmem = pl.BlockSpec(memory_space=pltpu.VMEM)
    limit = pltpu.CompilerParams(vmem_limit_bytes=VMEM_LIMIT)
    owners = fetch_owner[:, 0]
    fetch_count = owners.shape[0]
    first_slot = narrow_pos * fetch_count
    slot_ids = first_slot + jnp.arange(fetch_count, dtype=jnp.int32)
    tile_hit = jnp.any(tile_negs[:, :, None] == slot_ids[None, None, :], axis=1)
    tiles = tile_negs.shape[0]
    pos_slots = positives.reshape(tiles, QTILE) // BLOCK
    pos_hit = jnp.any(pos_slots[:, :, None] == slot_ids[None, None, :], axis=1)
    ask = pl.pallas_call(
        functools.partial(ask_kernel, (ring, narrow_count, blocks_here)),
        out_shape=jax.ShapeDtypeStruct((sources, QTILE), jnp.int32),
        in_specs=[smem] * 5,
        out_specs=smem,
        cost_estimate=pl.CostEstimate(flops=10**6, bytes_accessed=2**16, transcendentals=0),
        name="ask",
    )
    table = ask(
        jnp.stack([first_slot, core]),
        owners,
        fetch_local,
        tile_bits(tile_hit),
        tile_bits(jnp.logical_or(tile_hit, pos_hit)),
    )
    table = lax.all_to_all(table, SAME_CORE, 0, 0, tiled=True)

    first_row = narrow_pos * own_rows
    lse_own = lax.dynamic_slice_in_dim(lse_shift, first_row, own_rows, 0)
    loss_own = lax.dynamic_slice_in_dim(loss_weight, first_row, own_rows, 0)
    pos_own = lax.dynamic_slice_in_dim(positives, first_row, own_rows, 0)
    lse_full = lse_own + math.log(fetch_count * narrow_count * BLOCK)
    shift = jnp.log2(loss_own) - lse_full * math.log2(math.e)
    per_query = jnp.concatenate([shift, loss_own, pos_own.astype(jnp.float32), jnp.zeros_like(shift)])
    per_query = jnp.broadcast_to(per_query.reshape(8, QTILE)[None], (sources, 8, QTILE))
    rows = lax.all_to_all(per_query, SAME_CORE, 0, 0, tiled=True)
    rows = jnp.concatenate([rows, jnp.full((1, 8, QTILE), -1.0, jnp.float32)], axis=0)

    halves = []
    for h in range(2):
        part = queries[h * QTILE : (h + 1) * QTILE]
        spread = jnp.broadcast_to(part[None], (sources, QTILE, feat_width))
        part = lax.all_to_all(spread, SAME_CORE, 0, 0, tiled=True)
        halves.append(jnp.concatenate([part, jnp.zeros((1, QTILE, feat_width), part.dtype)]))

    held_shape = jax.ShapeDtypeStruct((2 * blocks_here, feat_width, BLOCK), jnp.bfloat16)
    turn = pl.pallas_call(
        turn_kernel,
        out_shape=(held_shape, held_shape),
        in_specs=[vmem, vmem],
        out_specs=(vmem, vmem),
        compiler_params=limit,
        cost_estimate=pl.CostEstimate(flops=10**9, bytes_accessed=2**24, transcendentals=0),
        name="turn",
    )
    blocks, turned = turn(held, mate_held)
    most = sources * PLACES * (tiles // 2) + 4 * UNROLL
    list_shape = jax.ShapeDtypeStruct((most,), jnp.int32)
    entries = sources // 4 * PLACES
    listing = pl.pallas_call(
        list_kernel,
        out_shape=(list_shape, list_shape, jax.ShapeDtypeStruct((2,), jnp.int32)),
        in_specs=[smem],
        out_specs=(smem, smem, smem),
        scratch_shapes=[pltpu.SMEM((entries,), jnp.int32)] * 3,
        cost_estimate=pl.CostEstimate(flops=10**9, bytes_accessed=2**20, transcendentals=0),
        name="listing",
    )
    *items, counts = listing(table)

    acc_shape = jax.ShapeDtypeStruct((2 * blocks_here, BLOCK, feat_width), jnp.float32)
    grad_shape = jax.ShapeDtypeStruct((sources, QTILE, feat_width), jnp.bfloat16)
    own_shape = jax.ShapeDtypeStruct((blocks_here, BLOCK, feat_width), jnp.float32)
    mate_shape = jax.ShapeDtypeStruct((blocks_here, BLOCK, feat_width), jnp.bfloat16)
    scratch = [
        pltpu.VMEM((sources + 1, feat_width, QTILE), jnp.bfloat16),
        pltpu.VMEM((sources + 1, feat_width, QTILE), jnp.float32),
        pltpu.VMEM((UNROLL, BLOCK, 2 * QTILE), jnp.float32),
        pltpu.VMEM((UNROLL, BLOCK, 2 * QTILE), jnp.bfloat16),
    ]
    cost = pl.CostEstimate(flops=2 * 10**10, bytes_accessed=2**25, transcendentals=10**7)
    chunk_0 = pl.pallas_call(
        functools.partial(chunk_kernel, 0, True, False),
        out_shape=(grad_shape, acc_shape),
        in_specs=[smem, smem, vmem, vmem, vmem, vmem],
        out_specs=(vmem, vmem),
        scratch_shapes=scratch,
        compiler_params=limit,
        cost_estimate=cost,
        name="chunk_0",
    )
    grad_0, acc = chunk_0(items[0], counts, rows, halves[0], blocks, turned)
    chunk_1 = pl.pallas_call(
        functools.partial(chunk_kernel, 1, False, True),
        out_shape=(grad_shape, own_shape, mate_shape),
        in_specs=[smem, smem, vmem, vmem, vmem, vmem, pl.BlockSpec(memory_space=pl.ANY)],
        out_specs=(vmem, vmem, vmem),
        scratch_shapes=scratch + [pltpu.VMEM(acc_shape.shape, jnp.float32), pltpu.SemaphoreType.DMA],
        compiler_params=limit,
        cost_estimate=cost,
        name="chunk_1",
    )
    grad_1, own_grad, mate_grad = chunk_1(items[1], counts, rows, halves[1], blocks, turned, acc)
    sums = []
    for part in (grad_0, grad_1):
        came = lax.all_to_all(part, SAME_CORE, 0, 0, tiled=True)
        sums.append(jnp.sum(came.astype(jnp.float32), axis=0))
    query_grad = jnp.concatenate(sums)
    from_mate = lax.ppermute(mate_grad, "c", [(0, 1), (1, 0)])
    held_grad = own_grad + from_mate.astype(jnp.float32)
    back = [
        lax.ppermute(held_grad[at].astype(jnp.bfloat16), axis, [(j, i) for i, j in way])
        for at, (axis, way) in zip(slabs, ways)
    ]
    index_grad = jnp.concatenate([held_grad[:KEPT]] + [part.astype(jnp.float32) for part in back])
    return (query_grad, index_grad.reshape(blocks_here * BLOCK, feat_width))


def solution(mesh):
    wide, narrow = mesh.devices.shape
    split = Mesh(mesh.devices.reshape(wide // 2, 2, 4, narrow // 4), ("y", "c", "z", "x"))
    every = ("y", "c", "z", "x")
    group = ("y", "c")
    in_specs = (
        P(every, None),
        P(every, None),
        P(group),
        P(group),
        P(group),
        P(group, None),
        P(every, None),
        P(every),
    )
    out_specs = (P(every, None), P(every, None))
    return jax.shard_map(shard_work, mesh=split, in_specs=in_specs, out_specs=out_specs, check_vma=False)
```

```python
import functools
import math

import jax
import jax.numpy as jnp
from jax import lax
from jax.experimental import pallas as pl
from jax.experimental.pallas import tpu as pltpu
from jax.sharding import Mesh
from jax.sharding import PartitionSpec as P


BLOCK = 128
QTILE = 128
CAP = 2
SAME_CORE = ("y", "z", "x")
NARROW = ("z", "x")
KEPT = 16
SLAB = 8
STEPS = (("x", 1), ("x", -1), ("y", 1), ("y", -1), ("z", 1), ("z", -1))
PLACES = 2 * CAP * (1 + len(STEPS))
FIELDS = 6
COUNT_AT = PLACES * FIELDS
DEAD = -1e30
UNROLL = 8
VMEM_LIMIT = 60 * 1024 * 1024


def tile_bits(flags):
    places = jnp.arange(flags.shape[0], dtype=jnp.int32)[:, None]
    return jnp.sum(jnp.left_shift(flags.astype(jnp.int32), places), axis=0)


def ask_kernel(sizes, where, owner, local, hits, lives, table):
    ring, narrow_count, blocks_here = sizes
    first_slot, core = where[0], where[1]

    def clear(d, carry):
        table[d, COUNT_AT] = 0
        return carry

    lax.fori_loop(0, table.shape[0], clear, 0)

    def ask(j, carry):
        own, block = owner[j], local[j]
        wide = own // narrow_count
        narrow = own % narrow_count
        turn = jnp.where(block < KEPT, -1, (block - KEPT) // SLAB)
        spot = {"y": wide // 2, "z": narrow // ring, "x": narrow % ring}
        for k, (axis, shift) in enumerate(STEPS):
            spot[axis] = spot[axis] + jnp.where(turn == k, shift + ring, 0)
        dest = ((spot["y"] % ring) * ring + spot["z"] % ring) * ring + spot["x"] % ring
        place = table[dest, COUNT_AT]
        table[dest, COUNT_AT] = place + 1
        at = place * FIELDS
        table[dest, at] = jnp.where(wide % 2 == core, 0, blocks_here) + block
        table[dest, at + 1] = first_slot + j
        table[dest, at + 2] = hits[j] & 0xFFFF
        table[dest, at + 3] = (hits[j] >> 16) & 0xFFFF
        table[dest, at + 4] = lives[j] & 0xFFFF
        table[dest, at + 5] = (lives[j] >> 16) & 0xFFFF
        return carry

    lax.fori_loop(0, owner.shape[0], ask, 0)


def list_kernel(table, first_items, second_items, counts, live, base, hits):
    groups = 4
    sources = table.shape[0]
    in_group = sources // groups
    dead = jnp.int32(sources)
    lists = (first_items, second_items)

    def group_entries(group, cursor):
        def source_entries(n, count):
            src = group * in_group + n

            def place_entry(place, count):
                at = place * FIELDS
                base[count] = (table[src, at] << 7) | (table[src, at + 1] << 15)
                hits[count] = table[src, at + 2] | (table[src, at + 3] << 16)
                live[count] = table[src, at + 4] | (table[src, at + 5] << 16)
                return count + 1

            return lax.fori_loop(0, table[src, COUNT_AT], place_entry, count)

        entries = lax.fori_loop(0, in_group, source_entries, jnp.int32(0))

        def entry_items(e, cursor):
            start = base[e] + group * in_group
            alive = live[e]
            hit = hits[e]
            empty = base[e] + dead
            out = []
            for h, at in enumerate(cursor):
                for n in range(in_group):
                    bit = 2 * n + h
                    named = (hit << (25 - bit)) if bit <= 25 else (hit >> (bit - 25))
                    lists[h][at] = (start + n) | (named & (1 << 25))
                    at = at + ((alive >> bit) & 1)
                lists[h][at] = empty
                out.append(at + (at & 1))
            return tuple(out)

        return lax.fori_loop(0, entries, entry_items, cursor)

    ends = lax.fori_loop(0, groups, group_entries, (jnp.int32(0), jnp.int32(0)))
    for h in range(2):
        for i in range(4 * UNROLL):
            lists[h][ends[h] + i] = dead
        counts[h] = (ends[h] + 2 * UNROLL - 1) // (2 * UNROLL)


def chunk_kernel(h, last, items, counts, rows_in, q_in, own_in, mate_in, *rest):
    if last:
        earlier_in, query_out, own_out, mate_out, block_acc, earlier = rest[:6]
    else:
        query_out, block_acc = rest[:2]
    rows, q, blocks, query_acc, scores, sems = rest[-6:]
    scale = 2.0 / math.sqrt(q.shape[2])
    factor = scale * math.log2(math.e)
    tiles = q_in.shape[0]
    here = own_in.shape[0]
    loads = [
        pltpu.make_async_copy(q_in, q.at[pl.ds(0, tiles)], sems.at[0]),
        pltpu.make_async_copy(own_in, blocks.at[pl.ds(0, here)], sems.at[1]),
        pltpu.make_async_copy(mate_in, blocks.at[pl.ds(here, here)], sems.at[2]),
        pltpu.make_async_copy(rows_in, rows.at[pl.ds(0, tiles)], sems.at[3]),
    ]
    if last:
        summed = pltpu.make_async_copy(earlier_in, earlier, sems.at[4])
    for load in loads:
        load.start()
    if last:
        summed.start()
    zero = jnp.zeros((BLOCK, QTILE), jnp.float32)
    q[tiles] = zero.astype(q.dtype)
    rows[tiles] = jnp.full(rows.shape[1:], -1.0, jnp.float32)
    query_acc[tiles] = zero

    def clear_query(t, carry):
        query_acc[t] = zero
        return carry

    def clear_block(b, carry):
        block_acc[b] = zero
        return carry

    lax.fori_loop(0, tiles, clear_query, 0, unroll=4)
    lax.fori_loop(0, 2 * here, clear_block, 0, unroll=4)
    scores[...] = jnp.zeros_like(scores)
    for load in loads:
        load.wait()

    column = lax.broadcasted_iota(jnp.int32, (BLOCK, QTILE), 0)

    def tile_of(word):
        return word & 127

    def block_of(word):
        return (word >> 7) & 127

    def block_grads(words, grad):
        block = block_of(words[0])
        t1, t2 = tile_of(words[0]), tile_of(words[1])
        both = jnp.concatenate([q[t1], q[t2]], axis=0)
        to_block = jnp.dot(grad, both, preferred_element_type=jnp.float32)
        part = lax.dot_general(
            blocks[block], grad, (((0,), (0,)), ((), ())), preferred_element_type=jnp.float32
        )
        block_acc[block] += to_block
        sum1 = query_acc[t1] + part[:, :QTILE]
        sum2 = query_acc[t2] + part[:, QTILE:]
        query_acc[t1] = sum1
        query_acc[t2] = sum2

    def logit_grads(words, scores):
        slot = (words[0] >> 15) & 1023
        halves = []
        for side, word in enumerate(words):
            tile = tile_of(word)
            hit = (word >> 25) & 1
            shift = rows[tile, pl.ds(h, 1), :]
            loss = rows[tile, pl.ds(2 + h, 1), :]
            positive = rows[tile, pl.ds(4 + h, 1), :].astype(jnp.int32)
            mine = (positive >> 7) == slot
            shift = jnp.where(jnp.logical_or(mine, hit > 0), shift, DEAD)
            target = jnp.where(mine, positive & 127, -1)
            at = slice(side * QTILE, (side + 1) * QTILE)
            terms = jnp.exp2(scores[:, at] * factor + shift)
            terms = terms - jnp.where(column == target, loss, 0.0)
            halves.append(terms.astype(jnp.bfloat16))
        return jnp.concatenate(halves, axis=1)

    def next_scores(words):
        both = jnp.concatenate([q[tile_of(words[0])], q[tile_of(words[1])]], axis=0)
        return lax.dot_general(
            blocks[block_of(words[0])], both, (((1,), (1,)), ((), ())), preferred_element_type=jnp.float32
        )

    def step(i, coming):
        starting = tuple((items[2 * (UNROLL * i + u)], items[2 * (UNROLL * i + u) + 1]) for u in range(UNROLL))
        for u in range(UNROLL):
            grad = logit_grads(coming[u], scores[u])
            block_grads(coming[u], grad)
            scores[u] = next_scores(starting[u])
        return starting

    dead = jnp.int32(tiles)
    lax.fori_loop(0, counts[h] + 1, step, ((dead, dead),) * UNROLL)

    def finish(t, carry):
        query_out[t] = (query_acc[t] * scale).T.astype(jnp.bfloat16)
        return carry

    lax.fori_loop(0, tiles, finish, 0, unroll=4)
    if last:
        summed.wait()

        def deliver(b, carry):
            own_out[b] = (block_acc[b] + earlier[b]) * scale
            mate_out[b] = ((block_acc[b + here] + earlier[b + here]) * scale).astype(jnp.bfloat16)
            return carry

        lax.fori_loop(0, here, deliver, 0, unroll=2)


def shard_work(
    queries, index_rows, lse_shift, loss_weight, positives, tile_negs, fetch_owner, fetch_local
):
    narrow_count = lax.axis_size(NARROW)
    sources = lax.axis_size(SAME_CORE)
    core = lax.axis_index("c")
    narrow_pos = lax.axis_index(NARROW)
    feat_width = queries.shape[1]
    own_rows = queries.shape[0]
    blocks_here = index_rows.shape[0] // BLOCK
    stored = index_rows.reshape(blocks_here, BLOCK, feat_width)
    halves = []
    for h in range(2):
        part = queries[h * QTILE : (h + 1) * QTILE]
        spread = jnp.broadcast_to(part[None], (sources, QTILE, feat_width))
        halves.append(lax.all_to_all(spread, SAME_CORE, 0, 0, tiled=True))
    ring = lax.axis_size("x")
    ways = []
    for axis, shift in STEPS:
        size = lax.axis_size(axis)
        ways.append((axis, [(i, (i + shift) % size) for i in range(size)]))
    slabs = [slice(KEPT + SLAB * k, KEPT + SLAB * (k + 1)) for k in range(len(STEPS))]
    lent = [lax.ppermute(stored[at], axis, way) for at, (axis, way) in zip(slabs, ways)]
    held = jnp.concatenate([stored[:KEPT]] + lent)
    mate_held = lax.ppermute(held, "c", [(0, 1), (1, 0)])

    smem = pl.BlockSpec(memory_space=pltpu.SMEM)
    vmem = pl.BlockSpec(memory_space=pltpu.VMEM)
    limit = pltpu.CompilerParams(vmem_limit_bytes=VMEM_LIMIT)
    owners = fetch_owner[:, 0]
    fetch_count = owners.shape[0]
    first_slot = narrow_pos * fetch_count
    slot_ids = first_slot + jnp.arange(fetch_count, dtype=jnp.int32)
    tile_hit = jnp.any(tile_negs[:, :, None] == slot_ids[None, None, :], axis=1)
    tiles = tile_negs.shape[0]
    pos_slots = positives.reshape(tiles, QTILE) // BLOCK
    pos_hit = jnp.any(pos_slots[:, :, None] == slot_ids[None, None, :], axis=1)
    ask = pl.pallas_call(
        functools.partial(ask_kernel, (ring, narrow_count, blocks_here)),
        out_shape=jax.ShapeDtypeStruct((sources, 2 * QTILE), jnp.int32),
        in_specs=[smem] * 5,
        out_specs=smem,
        cost_estimate=pl.CostEstimate(flops=10**6, bytes_accessed=2**16, transcendentals=0),
        name="ask",
    )
    table = ask(
        jnp.stack([first_slot, core]),
        owners,
        fetch_local,
        tile_bits(tile_hit),
        tile_bits(jnp.logical_or(tile_hit, pos_hit)),
    )
    first_row = narrow_pos * own_rows
    lse_own = lax.dynamic_slice_in_dim(lse_shift, first_row, own_rows, 0)
    loss_own = lax.dynamic_slice_in_dim(loss_weight, first_row, own_rows, 0)
    pos_own = lax.dynamic_slice_in_dim(positives, first_row, own_rows, 0)
    lse_full = lse_own + math.log(fetch_count * narrow_count * BLOCK)
    shift = jnp.log2(loss_own) - lse_full * math.log2(math.e)
    per_query = jnp.concatenate([shift, loss_own, pos_own.astype(jnp.float32)]).reshape(6, QTILE)
    per_query = jnp.broadcast_to(per_query[None], (sources, 6, QTILE))
    packed = table.astype(jnp.float32).reshape(sources, 2, QTILE)
    packed = jnp.concatenate([per_query, packed], axis=1)
    rows = lax.all_to_all(packed, SAME_CORE, 0, 0, tiled=True)
    table = rows[:, 6:].astype(jnp.int32).reshape(sources, 2 * QTILE)
    most = sources * PLACES * (tiles // 2) + 4 * UNROLL
    list_shape = jax.ShapeDtypeStruct((most,), jnp.int32)
    entries = sources // 4 * PLACES
    listing = pl.pallas_call(
        list_kernel,
        out_shape=(list_shape, list_shape, jax.ShapeDtypeStruct((2,), jnp.int32)),
        in_specs=[smem],
        out_specs=(smem, smem, smem),
        scratch_shapes=[pltpu.SMEM((entries,), jnp.int32)] * 3,
        cost_estimate=pl.CostEstimate(flops=10**9, bytes_accessed=2**20, transcendentals=0),
        name="listing",
    )
    *items, counts = listing(table)

    acc_shape = jax.ShapeDtypeStruct((2 * blocks_here, BLOCK, feat_width), jnp.float32)
    grad_shape = jax.ShapeDtypeStruct((sources, QTILE, feat_width), jnp.bfloat16)
    own_shape = jax.ShapeDtypeStruct((blocks_here, BLOCK, feat_width), jnp.float32)
    mate_shape = jax.ShapeDtypeStruct((blocks_here, BLOCK, feat_width), jnp.bfloat16)

    def scratch(extra):
        return extra + [
            pltpu.VMEM((sources + 1, 8, QTILE), jnp.float32),
            pltpu.VMEM((sources + 1, QTILE, feat_width), jnp.bfloat16),
            pltpu.VMEM((2 * blocks_here, BLOCK, feat_width), jnp.bfloat16),
            pltpu.VMEM((sources + 1, feat_width, QTILE), jnp.float32),
            pltpu.VMEM((UNROLL, BLOCK, 2 * QTILE), jnp.float32),
            pltpu.SemaphoreType.DMA((5,)),
        ]

    hbm = pl.BlockSpec(memory_space=pl.ANY)
    cost = pl.CostEstimate(flops=2 * 10**10, bytes_accessed=2**25, transcendentals=10**7)
    chunk_0 = pl.pallas_call(
        functools.partial(chunk_kernel, 0, False),
        out_shape=(grad_shape, acc_shape),
        in_specs=[smem, smem] + [hbm] * 4,
        out_specs=(vmem, vmem),
        scratch_shapes=scratch([]),
        compiler_params=limit,
        cost_estimate=cost,
        name="chunk_0",
    )
    grad_0, acc = chunk_0(items[0], counts, rows, halves[0], held, mate_held)
    chunk_1 = pl.pallas_call(
        functools.partial(chunk_kernel, 1, True),
        out_shape=(grad_shape, own_shape, mate_shape),
        in_specs=[smem, smem] + [hbm] * 5,
        out_specs=(vmem, vmem, vmem),
        scratch_shapes=scratch([pltpu.VMEM(acc_shape.shape, jnp.float32)] * 2),
        compiler_params=limit,
        cost_estimate=cost,
        name="chunk_1",
    )
    grad_1, own_grad, mate_grad = chunk_1(items[1], counts, rows, halves[1], held, mate_held, acc)
    sums = []
    for part in (grad_0, grad_1):
        came = lax.all_to_all(part, SAME_CORE, 0, 0, tiled=True)
        sums.append(jnp.sum(came.astype(jnp.float32), axis=0))
    query_grad = jnp.concatenate(sums)
    from_mate = lax.ppermute(mate_grad, "c", [(0, 1), (1, 0)])
    held_grad = own_grad + from_mate.astype(jnp.float32)
    back = [
        lax.ppermute(held_grad[at].astype(jnp.bfloat16), axis, [(j, i) for i, j in way])
        for at, (axis, way) in zip(slabs, ways)
    ]
    index_grad = jnp.concatenate([held_grad[:KEPT]] + [part.astype(jnp.float32) for part in back])
    return (query_grad, index_grad.reshape(blocks_here * BLOCK, feat_width))


def solution(mesh):
    wide, narrow = mesh.devices.shape
    split = Mesh(mesh.devices.reshape(wide // 2, 2, 4, narrow // 4), ("y", "c", "z", "x"))
    every = ("y", "c", "z", "x")
    group = ("y", "c")
    in_specs = (
        P(every, None),
        P(every, None),
        P(group),
        P(group),
        P(group),
        P(group, None),
        P(every, None),
        P(every),
    )
    out_specs = (P(every, None), P(every, None))
    return jax.shard_map(shard_work, mesh=split, in_specs=in_specs, out_specs=out_specs, check_vma=False)
```

```python
import functools
import math

import jax
import jax.numpy as jnp
from jax import lax
from jax.experimental import pallas as pl
from jax.experimental.pallas import tpu as pltpu
from jax.sharding import Mesh
from jax.sharding import PartitionSpec as P


BLOCK = 128
QTILE = 128
CAP = 2
SAME_CORE = ("y", "z", "x")
NARROW = ("z", "x")
KEPT = 16
SLAB = 8
STEPS = (("x", 1), ("x", -1), ("y", 1), ("y", -1), ("z", 1), ("z", -1))
PLACES = 2 * CAP * (1 + len(STEPS))
FIELDS = 6
COUNT_AT = PLACES * FIELDS
DEAD = -1e30
UNROLL = 12
VMEM_LIMIT = 60 * 1024 * 1024


def tile_bits(flags):
    places = jnp.arange(flags.shape[0], dtype=jnp.int32)[:, None]
    return jnp.sum(jnp.left_shift(flags.astype(jnp.int32), places), axis=0)


def ask_kernel(sizes, where, owner, local, hits, lives, table):
    ring, narrow_count, blocks_here = sizes
    ring_bits, narrow_bits = ring.bit_length() - 1, narrow_count.bit_length() - 1
    slab_bits = SLAB.bit_length() - 1
    first_slot, core = where[0], where[1]

    def clear(d, carry):
        table[d, COUNT_AT] = 0
        return carry

    lax.fori_loop(0, table.shape[0], clear, 0, unroll=8)

    def ask(j, carry):
        own, block = owner[j], local[j]
        wide = own >> narrow_bits
        narrow = own & (narrow_count - 1)
        turn = (block - KEPT) >> slab_bits
        spot = {"y": wide >> 1, "z": narrow >> ring_bits, "x": narrow & (ring - 1)}
        for k, (axis, shift) in enumerate(STEPS):
            spot[axis] = spot[axis] + jnp.where(turn == k, shift + ring, 0)
        edge = ring - 1
        dest = ((spot["y"] & edge) << (2 * ring_bits)) | ((spot["z"] & edge) << ring_bits) | (spot["x"] & edge)
        place = table[dest, COUNT_AT]
        table[dest, COUNT_AT] = place + 1
        at = place * FIELDS
        table[dest, at] = jnp.where((wide & 1) == core, 0, blocks_here) + block
        table[dest, at + 1] = first_slot + j
        table[dest, at + 2] = hits[j] & 0xFFFF
        table[dest, at + 3] = (hits[j] >> 16) & 0xFFFF
        table[dest, at + 4] = lives[j] & 0xFFFF
        table[dest, at + 5] = (lives[j] >> 16) & 0xFFFF
        return carry

    lax.fori_loop(0, owner.shape[0], ask, 0, unroll=4)


def list_kernel(table, first_items, second_items, counts, base, hits, live):
    groups = 4
    sources = table.shape[0]
    in_group = sources // groups
    dead = jnp.int32(sources)
    lists = (first_items, second_items)

    def group_entries(group, cursor):
        begin = cursor[2]

        def source_entries(n, count):
            src = group * in_group + n

            def place_entry(place, count):
                at = place * FIELDS
                base[count] = table[src, at] | (table[src, at + 1] << 7)
                hits[count] = table[src, at + 2] | (table[src, at + 3] << 16)
                live[count] = table[src, at + 4] | (table[src, at + 5] << 16)
                return count + 1

            return lax.fori_loop(0, table[src, COUNT_AT], place_entry, count)

        finish = lax.fori_loop(0, in_group, source_entries, begin)

        def entry_items(e, ends):
            start = (e << 7) + group * in_group
            alive = live[e]
            empty = (e << 7) + dead
            out = []
            for h, at in enumerate(ends):
                for n in range(in_group):
                    lists[h][at] = start + n
                    at = at + ((alive >> (2 * n + h)) & 1)
                lists[h][at] = empty
                out.append(at + (at & 1))
            return tuple(out)

        ends = lax.fori_loop(begin, finish, entry_items, cursor[:2])
        return ends + (finish,)

    zero = jnp.int32(0)
    base[0] = zero
    hits[0] = zero
    ends = lax.fori_loop(0, groups, group_entries, (zero, zero, zero))
    for h in range(2):
        for i in range(4 * UNROLL):
            lists[h][ends[h] + i] = dead
        counts[h] = (ends[h] + 2 * UNROLL - 1) // (2 * UNROLL)


def chunk_kernel(h, last, items, counts, base, hits, rows_in, q_in, own_in, mate_in, *rest):
    if last:
        earlier_in, query_out, own_out, mate_out, block_acc, earlier = rest[:6]
    else:
        query_out, block_acc = rest[:2]
    rows, q, blocks, query_acc, scores, sems = rest[-6:]
    scale = 2.0 / math.sqrt(q.shape[2])
    factor = scale * math.log2(math.e)
    tiles = q_in.shape[0]
    here = own_in.shape[0]
    loads = [
        pltpu.make_async_copy(q_in, q.at[pl.ds(0, tiles)], sems.at[0]),
        pltpu.make_async_copy(own_in, blocks.at[pl.ds(0, here)], sems.at[1]),
        pltpu.make_async_copy(mate_in, blocks.at[pl.ds(here, here)], sems.at[2]),
        pltpu.make_async_copy(rows_in, rows.at[pl.ds(0, tiles)], sems.at[3]),
    ]
    if last:
        summed = pltpu.make_async_copy(earlier_in, earlier, sems.at[4])
    for load in loads:
        load.start()
    if last:
        summed.start()
    zero = jnp.zeros((BLOCK, QTILE), jnp.float32)
    q[tiles] = zero.astype(q.dtype)
    rows[tiles] = jnp.full(rows.shape[1:], -1.0, jnp.float32)
    query_acc[tiles] = zero

    def clear_query(t, carry):
        query_acc[t] = zero
        return carry

    def clear_block(b, carry):
        block_acc[b] = zero
        return carry

    lax.fori_loop(0, tiles, clear_query, 0, unroll=4)
    lax.fori_loop(0, 2 * here, clear_block, 0, unroll=4)
    scores[...] = jnp.zeros_like(scores)
    for load in loads:
        load.wait()

    column = lax.broadcasted_iota(jnp.int32, (BLOCK, QTILE), 0)

    def tile_of(word):
        return word & 127

    def block_of(word):
        return base[word >> 7] & 127

    def block_grads(words, grad):
        block = block_of(words[0])
        t1, t2 = tile_of(words[0]), tile_of(words[1])
        both = jnp.concatenate([q[t1], q[t2]], axis=0)
        to_block = jnp.dot(grad, both, preferred_element_type=jnp.float32)
        part = lax.dot_general(
            blocks[block], grad, (((0,), (0,)), ((), ())), preferred_element_type=jnp.float32
        )
        block_acc[block] += to_block
        sum1 = query_acc[t1] + part[:, :QTILE]
        sum2 = query_acc[t2] + part[:, QTILE:]
        query_acc[t1] = sum1
        query_acc[t2] = sum2

    def logit_grads(words, scores):
        slot = base[words[0] >> 7] >> 7
        halves = []
        for side, word in enumerate(words):
            tile = tile_of(word)
            hit = (hits[word >> 7] >> (2 * (tile & (tiles // 4 - 1)) + h)) & 1
            shift = rows[tile, pl.ds(h, 1), :]
            loss = rows[tile, pl.ds(2 + h, 1), :]
            positive = rows[tile, pl.ds(4 + h, 1), :].astype(jnp.int32)
            mine = (positive >> 7) == slot
            shift = jnp.where(jnp.logical_or(mine, hit > 0), shift, DEAD)
            target = jnp.where(mine, positive & 127, -1)
            at = slice(side * QTILE, (side + 1) * QTILE)
            terms = jnp.exp2(scores[:, at] * factor + shift)
            terms = terms - jnp.where(column == target, loss, 0.0)
            halves.append(terms.astype(jnp.bfloat16))
        return jnp.concatenate(halves, axis=1)

    def next_scores(words):
        both = jnp.concatenate([q[tile_of(words[0])], q[tile_of(words[1])]], axis=0)
        return lax.dot_general(
            blocks[block_of(words[0])], both, (((1,), (1,)), ((), ())), preferred_element_type=jnp.float32
        )

    def step(i, coming):
        starting = tuple((items[2 * (UNROLL * i + u)], items[2 * (UNROLL * i + u) + 1]) for u in range(UNROLL))
        for u in range(UNROLL):
            grad = logit_grads(coming[u], scores[u])
            block_grads(coming[u], grad)
            scores[u] = next_scores(starting[u])
        return starting

    dead = jnp.int32(tiles)
    lax.fori_loop(0, counts[h] + 1, step, ((dead, dead),) * UNROLL)

    def finish(t, carry):
        query_out[t] = (query_acc[t] * scale).T.astype(jnp.bfloat16)
        return carry

    lax.fori_loop(0, tiles, finish, 0, unroll=4)
    if last:
        summed.wait()

        def deliver(b, carry):
            own_out[b] = (block_acc[b] + earlier[b]) * scale
            mate_out[b] = ((block_acc[b + here] + earlier[b + here]) * scale).astype(jnp.bfloat16)
            return carry

        lax.fori_loop(0, here, deliver, 0, unroll=2)


def assemble_kernel(kept, *rest):
    *back, out = rest
    out[pl.ds(0, KEPT)] = kept[...]
    for k, part in enumerate(back):
        out[pl.ds(KEPT + SLAB * k, SLAB)] = part[...].astype(jnp.float32)


def shard_work(
    queries, index_rows, lse_shift, loss_weight, positives, tile_negs, fetch_owner, fetch_local
):
    narrow_count = lax.axis_size(NARROW)
    sources = lax.axis_size(SAME_CORE)
    core = lax.axis_index("c")
    narrow_pos = lax.axis_index(NARROW)
    feat_width = queries.shape[1]
    own_rows = queries.shape[0]
    blocks_here = index_rows.shape[0] // BLOCK
    stored = index_rows.reshape(blocks_here, BLOCK, feat_width)
    halves = []
    for h in range(2):
        part = queries[h * QTILE : (h + 1) * QTILE]
        spread = jnp.broadcast_to(part[None], (sources, QTILE, feat_width))
        halves.append(lax.all_to_all(spread, SAME_CORE, 0, 0, tiled=True))
    ring = lax.axis_size("x")
    ways = []
    for axis, shift in STEPS:
        size = lax.axis_size(axis)
        ways.append((axis, [(i, (i + shift) % size) for i in range(size)]))
    slabs = [slice(KEPT + SLAB * k, KEPT + SLAB * (k + 1)) for k in range(len(STEPS))]
    lent = [lax.ppermute(stored[at], axis, way) for at, (axis, way) in zip(slabs, ways)]
    held = jnp.concatenate([stored[:KEPT]] + lent)
    mate_held = lax.ppermute(held, "c", [(0, 1), (1, 0)])

    smem = pl.BlockSpec(memory_space=pltpu.SMEM)
    vmem = pl.BlockSpec(memory_space=pltpu.VMEM)
    limit = pltpu.CompilerParams(vmem_limit_bytes=VMEM_LIMIT)
    owners = fetch_owner[:, 0]
    fetch_count = owners.shape[0]
    first_slot = narrow_pos * fetch_count
    slot_ids = first_slot + jnp.arange(fetch_count, dtype=jnp.int32)
    tile_hit = jnp.any(tile_negs[:, :, None] == slot_ids[None, None, :], axis=1)
    tiles = tile_negs.shape[0]
    pos_slots = positives.reshape(tiles, QTILE) // BLOCK
    pos_hit = jnp.any(pos_slots[:, :, None] == slot_ids[None, None, :], axis=1)
    ask = pl.pallas_call(
        functools.partial(ask_kernel, (ring, narrow_count, blocks_here)),
        out_shape=jax.ShapeDtypeStruct((sources, 2 * QTILE), jnp.int32),
        in_specs=[smem] * 5,
        out_specs=smem,
        cost_estimate=pl.CostEstimate(flops=10**6, bytes_accessed=2**16, transcendentals=0),
        name="ask",
    )
    table = ask(
        jnp.stack([first_slot, core]),
        owners,
        fetch_local,
        tile_bits(tile_hit),
        tile_bits(jnp.logical_or(tile_hit, pos_hit)),
    )
    first_row = narrow_pos * own_rows
    lse_own = lax.dynamic_slice_in_dim(lse_shift, first_row, own_rows, 0)
    loss_own = lax.dynamic_slice_in_dim(loss_weight, first_row, own_rows, 0)
    pos_own = lax.dynamic_slice_in_dim(positives, first_row, own_rows, 0)
    lse_full = lse_own + math.log(fetch_count * narrow_count * BLOCK)
    shift = jnp.log2(loss_own) - lse_full * math.log2(math.e)
    per_query = jnp.concatenate([shift, loss_own, pos_own.astype(jnp.float32)]).reshape(6, QTILE)
    per_query = jnp.broadcast_to(per_query[None], (sources, 6, QTILE))
    packed = table.astype(jnp.float32).reshape(sources, 2, QTILE)
    packed = jnp.concatenate([per_query, packed], axis=1)
    rows = lax.all_to_all(packed, SAME_CORE, 0, 0, tiled=True)
    table = rows[:, 6:].astype(jnp.int32).reshape(sources, 2 * QTILE)
    most = sources * PLACES * (tiles // 2) + 4 * UNROLL
    list_shape = jax.ShapeDtypeStruct((most,), jnp.int32)
    entry_shape = jax.ShapeDtypeStruct((sources * PLACES,), jnp.int32)
    listing = pl.pallas_call(
        list_kernel,
        out_shape=(list_shape, list_shape, jax.ShapeDtypeStruct((2,), jnp.int32), entry_shape, entry_shape),
        in_specs=[smem],
        out_specs=(smem,) * 5,
        scratch_shapes=[pltpu.SMEM(entry_shape.shape, jnp.int32)],
        cost_estimate=pl.CostEstimate(flops=10**9, bytes_accessed=2**20, transcendentals=0),
        name="listing",
    )
    *items, counts, base, hits = listing(table)

    acc_shape = jax.ShapeDtypeStruct((2 * blocks_here, BLOCK, feat_width), jnp.float32)
    grad_shape = jax.ShapeDtypeStruct((sources, QTILE, feat_width), jnp.bfloat16)
    own_shape = jax.ShapeDtypeStruct((blocks_here, BLOCK, feat_width), jnp.float32)
    mate_shape = jax.ShapeDtypeStruct((blocks_here, BLOCK, feat_width), jnp.bfloat16)

    def scratch(extra):
        return extra + [
            pltpu.VMEM((sources + 1, 8, QTILE), jnp.float32),
            pltpu.VMEM((sources + 1, QTILE, feat_width), jnp.bfloat16),
            pltpu.VMEM((2 * blocks_here, BLOCK, feat_width), jnp.bfloat16),
            pltpu.VMEM((sources + 1, feat_width, QTILE), jnp.float32),
            pltpu.VMEM((UNROLL, BLOCK, 2 * QTILE), jnp.float32),
            pltpu.SemaphoreType.DMA((5,)),
        ]

    hbm = pl.BlockSpec(memory_space=pl.ANY)
    cost = pl.CostEstimate(flops=2 * 10**10, bytes_accessed=2**25, transcendentals=10**7)
    chunk_0 = pl.pallas_call(
        functools.partial(chunk_kernel, 0, False),
        out_shape=(grad_shape, acc_shape),
        in_specs=[smem] * 4 + [hbm] * 4,
        out_specs=(vmem, vmem),
        scratch_shapes=scratch([]),
        compiler_params=limit,
        cost_estimate=cost,
        name="chunk_0",
    )
    grad_0, acc = chunk_0(items[0], counts, base, hits, rows, halves[0], held, mate_held)
    chunk_1 = pl.pallas_call(
        functools.partial(chunk_kernel, 1, True),
        out_shape=(grad_shape, own_shape, mate_shape),
        in_specs=[smem] * 4 + [hbm] * 5,
        out_specs=(vmem, vmem, vmem),
        scratch_shapes=scratch([pltpu.VMEM(acc_shape.shape, jnp.float32)] * 2),
        compiler_params=limit,
        cost_estimate=cost,
        name="chunk_1",
    )
    grad_1, own_grad, mate_grad = chunk_1(items[1], counts, base, hits, rows, halves[1], held, mate_held, acc)
    sums = []
    for part in (grad_0, grad_1):
        came = lax.all_to_all(part, SAME_CORE, 0, 0, tiled=True)
        sums.append(jnp.sum(came.astype(jnp.float32), axis=0))
    query_grad = jnp.concatenate(sums)
    from_mate = lax.ppermute(mate_grad, "c", [(0, 1), (1, 0)])
    held_grad = own_grad + from_mate.astype(jnp.float32)
    back = [
        lax.ppermute(held_grad[at].astype(jnp.bfloat16), axis, [(j, i) for i, j in way])
        for at, (axis, way) in zip(slabs, ways)
    ]
    assemble = pl.pallas_call(
        assemble_kernel,
        out_shape=own_shape,
        in_specs=[vmem] * (1 + len(back)),
        out_specs=vmem,
        compiler_params=limit,
        cost_estimate=pl.CostEstimate(flops=10**6, bytes_accessed=2**23, transcendentals=0),
        name="assemble",
    )
    index_grad = assemble(held_grad[:KEPT], *back)
    return (query_grad, index_grad.reshape(blocks_here * BLOCK, feat_width))


def solution(mesh):
    wide, narrow = mesh.devices.shape
    split = Mesh(mesh.devices.reshape(wide // 2, 2, 4, narrow // 4), ("y", "c", "z", "x"))
    every = ("y", "c", "z", "x")
    group = ("y", "c")
    in_specs = (
        P(every, None),
        P(every, None),
        P(group),
        P(group),
        P(group),
        P(group, None),
        P(every, None),
        P(every),
    )
    out_specs = (P(every, None), P(every, None))
    return jax.shard_map(shard_work, mesh=split, in_specs=in_specs, out_specs=out_specs, check_vma=False)
```

```python
import functools
import math

import jax
import jax.numpy as jnp
from jax import lax
from jax.experimental import pallas as pl
from jax.experimental.pallas import tpu as pltpu
from jax.sharding import Mesh
from jax.sharding import PartitionSpec as P


BLOCK = 128
QTILE = 128
CAP = 2
SAME_CORE = ("y", "z", "x")
NARROW = ("z", "x")
KEPT = 16
SLAB = 8
STEPS = (("x", 1), ("x", -1), ("y", 1), ("y", -1), ("z", 1), ("z", -1))
PLACES = 2 * CAP * (1 + len(STEPS))
FIELDS = 6
COUNT_AT = PLACES * FIELDS
DEAD = -1e30
UNROLL = 12
VMEM_LIMIT = 60 * 1024 * 1024


def tile_bits(flags):
    places = jnp.arange(flags.shape[0], dtype=jnp.int32)[:, None]
    return jnp.sum(jnp.left_shift(flags.astype(jnp.int32), places), axis=0)


def ask_kernel(sizes, where, owner, local, hits, lives, table):
    ring, narrow_count, blocks_here = sizes
    ring_bits, narrow_bits = ring.bit_length() - 1, narrow_count.bit_length() - 1
    slab_bits = SLAB.bit_length() - 1
    first_slot, core = where[0], where[1]

    def clear(d, carry):
        table[d, COUNT_AT] = 0
        return carry

    lax.fori_loop(0, table.shape[0], clear, 0, unroll=8)

    def ask(j, carry):
        own, block = owner[j], local[j]
        wide = own >> narrow_bits
        narrow = own & (narrow_count - 1)
        turn = (block - KEPT) >> slab_bits
        spot = {"y": wide >> 1, "z": narrow >> ring_bits, "x": narrow & (ring - 1)}
        for k, (axis, shift) in enumerate(STEPS):
            spot[axis] = spot[axis] + jnp.where(turn == k, shift + ring, 0)
        edge = ring - 1
        dest = ((spot["y"] & edge) << (2 * ring_bits)) | ((spot["z"] & edge) << ring_bits) | (spot["x"] & edge)
        place = table[dest, COUNT_AT]
        table[dest, COUNT_AT] = place + 1
        at = place * FIELDS
        table[dest, at] = jnp.where((wide & 1) == core, 0, blocks_here) + block
        table[dest, at + 1] = first_slot + j
        table[dest, at + 2] = hits[j] & 0xFFFF
        table[dest, at + 3] = (hits[j] >> 16) & 0xFFFF
        table[dest, at + 4] = lives[j] & 0xFFFF
        table[dest, at + 5] = (lives[j] >> 16) & 0xFFFF
        return carry

    lax.fori_loop(0, owner.shape[0], ask, 0, unroll=4)


def list_kernel(table, first_items, second_items, counts, base, hits, live):
    groups = 4
    sources = table.shape[0]
    in_group = sources // groups
    dead = jnp.int32(sources)
    lists = (first_items, second_items)

    def group_entries(group, cursor):
        begin = cursor[2]

        def source_entries(n, count):
            src = group * in_group + n

            def place_entry(place, count):
                at = place * FIELDS
                base[count] = table[src, at] | (table[src, at + 1] << 7)
                hits[count] = table[src, at + 2] | (table[src, at + 3] << 16)
                live[count] = table[src, at + 4] | (table[src, at + 5] << 16)
                return count + 1

            return lax.fori_loop(0, table[src, COUNT_AT], place_entry, count)

        finish = lax.fori_loop(0, in_group, source_entries, begin)

        def entry_items(e, ends):
            start = (e << 7) + group * in_group
            alive = live[e]
            empty = (e << 7) + dead
            out = []
            for h, at in enumerate(ends):
                for n in range(in_group):
                    lists[h][at] = start + n
                    at = at + ((alive >> (2 * n + h)) & 1)
                lists[h][at] = empty
                out.append(at + (at & 1))
            return tuple(out)

        ends = lax.fori_loop(begin, finish, entry_items, cursor[:2])
        return ends + (finish,)

    zero = jnp.int32(0)
    base[0] = zero
    hits[0] = zero
    ends = lax.fori_loop(0, groups, group_entries, (zero, zero, zero))
    for h in range(2):
        for i in range(4 * UNROLL):
            lists[h][ends[h] + i] = dead
        counts[h] = (ends[h] + 2 * UNROLL - 1) // (2 * UNROLL)


def chunk_kernel(h, last, items, counts, base, hits, rows_in, q_in, own_in, mate_in, *rest):
    if last:
        earlier_in, query_out, own_out, mate_out, block_acc, earlier = rest[:6]
    else:
        query_out, block_acc = rest[:2]
    rows, q, blocks, query_acc, scores, sems = rest[-6:]
    scale = 2.0 / math.sqrt(q.shape[2])
    factor = scale * math.log2(math.e)
    tiles = q_in.shape[0]
    here = own_in.shape[0]
    loads = [
        pltpu.make_async_copy(q_in, q.at[pl.ds(0, tiles)], sems.at[0]),
        pltpu.make_async_copy(own_in, blocks.at[pl.ds(0, here)], sems.at[1]),
        pltpu.make_async_copy(mate_in, blocks.at[pl.ds(here, here)], sems.at[2]),
        pltpu.make_async_copy(rows_in, rows.at[pl.ds(0, tiles)], sems.at[3]),
    ]
    if last:
        summed = pltpu.make_async_copy(earlier_in, earlier, sems.at[4])
    for load in loads:
        load.start()
    if last:
        summed.start()
    zero = jnp.zeros((BLOCK, QTILE), jnp.float32)
    q[tiles] = zero.astype(q.dtype)
    rows[tiles] = jnp.full(rows.shape[1:], -1.0, jnp.float32)
    query_acc[tiles] = zero

    def clear_query(t, carry):
        query_acc[t] = zero
        return carry

    def clear_block(b, carry):
        block_acc[b] = zero
        return carry

    lax.fori_loop(0, tiles, clear_query, 0, unroll=4)
    lax.fori_loop(0, 2 * here, clear_block, 0, unroll=4)
    scores[...] = jnp.zeros_like(scores)
    for load in loads:
        load.wait()

    column = lax.broadcasted_iota(jnp.int32, (BLOCK, QTILE), 0)

    def tile_of(word):
        return word & 127

    def block_of(word):
        return base[word >> 7] & 127

    def block_grads(words, grad):
        block = block_of(words[0])
        t1, t2 = tile_of(words[0]), tile_of(words[1])
        both = jnp.concatenate([q[t1], q[t2]], axis=0)
        to_block = jnp.dot(grad, both, preferred_element_type=jnp.float32)
        part = lax.dot_general(
            blocks[block], grad, (((0,), (0,)), ((), ())), preferred_element_type=jnp.float32
        )
        block_acc[block] += to_block
        sum1 = query_acc[t1] + part[:, :QTILE]
        sum2 = query_acc[t2] + part[:, QTILE:]
        query_acc[t1] = sum1
        query_acc[t2] = sum2

    def logit_grads(words, scores):
        slot = base[words[0] >> 7] >> 7
        halves = []
        for side, word in enumerate(words):
            tile = tile_of(word)
            hit = (hits[word >> 7] >> (2 * (tile & (tiles // 4 - 1)) + h)) & 1
            shift = rows[tile, pl.ds(h, 1), :]
            loss = rows[tile, pl.ds(2 + h, 1), :]
            positive = rows[tile, pl.ds(4 + h, 1), :].astype(jnp.int32)
            mine = (positive >> 7) == slot
            shift = jnp.where(jnp.logical_or(mine, hit > 0), shift, DEAD)
            target = jnp.where(mine, positive & 127, -1)
            at = slice(side * QTILE, (side + 1) * QTILE)
            terms = jnp.exp2(scores[:, at] * factor + shift)
            terms = terms - jnp.where(column == target, loss, 0.0)
            halves.append(terms.astype(jnp.bfloat16))
        return jnp.concatenate(halves, axis=1)

    def next_scores(words):
        both = jnp.concatenate([q[tile_of(words[0])], q[tile_of(words[1])]], axis=0)
        return lax.dot_general(
            blocks[block_of(words[0])], both, (((1,), (1,)), ((), ())), preferred_element_type=jnp.float32
        )

    def step(i, coming):
        starting = tuple((items[2 * (UNROLL * i + u)], items[2 * (UNROLL * i + u) + 1]) for u in range(UNROLL))
        for u in range(UNROLL):
            grad = logit_grads(coming[u], scores[u])
            block_grads(coming[u], grad)
            scores[u] = next_scores(starting[u])
        return starting

    dead = jnp.int32(tiles)
    lax.fori_loop(0, counts[h] + 1, step, ((dead, dead),) * UNROLL)

    def finish(t, carry):
        query_out[t] = (query_acc[t] * scale).T.astype(jnp.bfloat16)
        return carry

    lax.fori_loop(0, tiles, finish, 0, unroll=4)
    if last:
        summed.wait()

        def deliver(b, carry):
            own_out[b] = (block_acc[b] + earlier[b]) * scale
            mate_out[b] = ((block_acc[b + here] + earlier[b + here]) * scale).astype(jnp.bfloat16)
            return carry

        lax.fori_loop(0, here, deliver, 0, unroll=2)


def hold_kernel(counts, kept, *rest):
    *lent, out = rest

    @pl.when(counts[0] >= 0)
    def _():
        out[pl.ds(0, KEPT)] = kept[...]
        for k, part in enumerate(lent):
            out[pl.ds(KEPT + SLAB * k, SLAB)] = part[...]


def assemble_kernel(kept, *rest):
    *back, out = rest
    out[pl.ds(0, KEPT)] = kept[...]
    for k, part in enumerate(back):
        out[pl.ds(KEPT + SLAB * k, SLAB)] = part[...].astype(jnp.float32)


def shard_work(
    queries, index_rows, lse_shift, loss_weight, positives, tile_negs, fetch_owner, fetch_local
):
    narrow_count = lax.axis_size(NARROW)
    sources = lax.axis_size(SAME_CORE)
    core = lax.axis_index("c")
    narrow_pos = lax.axis_index(NARROW)
    feat_width = queries.shape[1]
    own_rows = queries.shape[0]
    blocks_here = index_rows.shape[0] // BLOCK
    stored = index_rows.reshape(blocks_here, BLOCK, feat_width)
    halves = []
    for h in range(2):
        part = queries[h * QTILE : (h + 1) * QTILE]
        spread = jnp.broadcast_to(part[None], (sources, QTILE, feat_width))
        halves.append(lax.all_to_all(spread, SAME_CORE, 0, 0, tiled=True))
    ring = lax.axis_size("x")
    ways = []
    for axis, shift in STEPS:
        size = lax.axis_size(axis)
        ways.append((axis, [(i, (i + shift) % size) for i in range(size)]))
    slabs = [slice(KEPT + SLAB * k, KEPT + SLAB * (k + 1)) for k in range(len(STEPS))]
    lent = [lax.ppermute(stored[at], axis, way) for at, (axis, way) in zip(slabs, ways)]
    kept = stored[:KEPT]
    smem = pl.BlockSpec(memory_space=pltpu.SMEM)
    vmem = pl.BlockSpec(memory_space=pltpu.VMEM)
    limit = pltpu.CompilerParams(vmem_limit_bytes=VMEM_LIMIT)
    owners = fetch_owner[:, 0]
    fetch_count = owners.shape[0]
    first_slot = narrow_pos * fetch_count
    slot_ids = first_slot + jnp.arange(fetch_count, dtype=jnp.int32)
    tile_hit = jnp.any(tile_negs[:, :, None] == slot_ids[None, None, :], axis=1)
    tiles = tile_negs.shape[0]
    pos_slots = positives.reshape(tiles, QTILE) // BLOCK
    pos_hit = jnp.any(pos_slots[:, :, None] == slot_ids[None, None, :], axis=1)
    ask = pl.pallas_call(
        functools.partial(ask_kernel, (ring, narrow_count, blocks_here)),
        out_shape=jax.ShapeDtypeStruct((sources, 2 * QTILE), jnp.int32),
        in_specs=[smem] * 5,
        out_specs=smem,
        cost_estimate=pl.CostEstimate(flops=10**6, bytes_accessed=2**16, transcendentals=0),
        name="ask",
    )
    table = ask(
        jnp.stack([first_slot, core]),
        owners,
        fetch_local,
        tile_bits(tile_hit),
        tile_bits(jnp.logical_or(tile_hit, pos_hit)),
    )
    first_row = narrow_pos * own_rows
    lse_own = lax.dynamic_slice_in_dim(lse_shift, first_row, own_rows, 0)
    loss_own = lax.dynamic_slice_in_dim(loss_weight, first_row, own_rows, 0)
    pos_own = lax.dynamic_slice_in_dim(positives, first_row, own_rows, 0)
    lse_full = lse_own + math.log(fetch_count * narrow_count * BLOCK)
    shift = jnp.log2(loss_own) - lse_full * math.log2(math.e)
    per_query = jnp.concatenate([shift, loss_own, pos_own.astype(jnp.float32)]).reshape(6, QTILE)
    per_query = jnp.broadcast_to(per_query[None], (sources, 6, QTILE))
    packed = table.astype(jnp.float32).reshape(sources, 2, QTILE)
    packed = jnp.concatenate([per_query, packed], axis=1)
    rows = lax.all_to_all(packed, SAME_CORE, 0, 0, tiled=True)
    table = rows[:, 6:].astype(jnp.int32).reshape(sources, 2 * QTILE)
    most = sources * PLACES * (tiles // 2) + 4 * UNROLL
    list_shape = jax.ShapeDtypeStruct((most,), jnp.int32)
    entry_shape = jax.ShapeDtypeStruct((sources * PLACES,), jnp.int32)
    listing = pl.pallas_call(
        list_kernel,
        out_shape=(list_shape, list_shape, jax.ShapeDtypeStruct((2,), jnp.int32), entry_shape, entry_shape),
        in_specs=[smem],
        out_specs=(smem,) * 5,
        scratch_shapes=[pltpu.SMEM(entry_shape.shape, jnp.int32)],
        cost_estimate=pl.CostEstimate(flops=10**9, bytes_accessed=2**20, transcendentals=0),
        name="listing",
    )
    *items, counts, base, hits = listing(table)
    hold = pl.pallas_call(
        hold_kernel,
        out_shape=jax.ShapeDtypeStruct(stored.shape, stored.dtype),
        in_specs=[smem] + [vmem] * (1 + len(lent)),
        out_specs=vmem,
        compiler_params=limit,
        cost_estimate=pl.CostEstimate(flops=10**6, bytes_accessed=2**22, transcendentals=0),
        name="hold",
    )
    held = hold(counts, kept, *lent)
    mate_held = lax.ppermute(held, "c", [(0, 1), (1, 0)])

    acc_shape = jax.ShapeDtypeStruct((2 * blocks_here, BLOCK, feat_width), jnp.float32)
    grad_shape = jax.ShapeDtypeStruct((sources, QTILE, feat_width), jnp.bfloat16)
    own_shape = jax.ShapeDtypeStruct((blocks_here, BLOCK, feat_width), jnp.float32)
    mate_shape = jax.ShapeDtypeStruct((blocks_here, BLOCK, feat_width), jnp.bfloat16)

    def scratch(extra):
        return extra + [
            pltpu.VMEM((sources + 1, 8, QTILE), jnp.float32),
            pltpu.VMEM((sources + 1, QTILE, feat_width), jnp.bfloat16),
            pltpu.VMEM((2 * blocks_here, BLOCK, feat_width), jnp.bfloat16),
            pltpu.VMEM((sources + 1, feat_width, QTILE), jnp.float32),
            pltpu.VMEM((UNROLL, BLOCK, 2 * QTILE), jnp.float32),
            pltpu.SemaphoreType.DMA((5,)),
        ]

    hbm = pl.BlockSpec(memory_space=pl.ANY)
    cost = pl.CostEstimate(flops=2 * 10**10, bytes_accessed=2**25, transcendentals=10**7)
    chunk_0 = pl.pallas_call(
        functools.partial(chunk_kernel, 0, False),
        out_shape=(grad_shape, acc_shape),
        in_specs=[smem] * 4 + [hbm] * 4,
        out_specs=(vmem, vmem),
        scratch_shapes=scratch([]),
        compiler_params=limit,
        cost_estimate=cost,
        name="chunk_0",
    )
    grad_0, acc = chunk_0(items[0], counts, base, hits, rows, halves[0], held, mate_held)
    chunk_1 = pl.pallas_call(
        functools.partial(chunk_kernel, 1, True),
        out_shape=(grad_shape, own_shape, mate_shape),
        in_specs=[smem] * 4 + [hbm] * 5,
        out_specs=(vmem, vmem, vmem),
        scratch_shapes=scratch([pltpu.VMEM(acc_shape.shape, jnp.float32)] * 2),
        compiler_params=limit,
        cost_estimate=cost,
        name="chunk_1",
    )
    grad_1, own_grad, mate_grad = chunk_1(items[1], counts, base, hits, rows, halves[1], held, mate_held, acc)
    sums = []
    for part in (grad_0, grad_1):
        came = lax.all_to_all(part, SAME_CORE, 0, 0, tiled=True)
        sums.append(jnp.sum(came.astype(jnp.float32), axis=0))
    query_grad = jnp.concatenate(sums)
    from_mate = lax.ppermute(mate_grad, "c", [(0, 1), (1, 0)])
    held_grad = own_grad + from_mate.astype(jnp.float32)
    back = [
        lax.ppermute(held_grad[at].astype(jnp.bfloat16), axis, [(j, i) for i, j in way])
        for at, (axis, way) in zip(slabs, ways)
    ]
    assemble = pl.pallas_call(
        assemble_kernel,
        out_shape=own_shape,
        in_specs=[vmem] * (1 + len(back)),
        out_specs=vmem,
        compiler_params=limit,
        cost_estimate=pl.CostEstimate(flops=10**6, bytes_accessed=2**23, transcendentals=0),
        name="assemble",
    )
    index_grad = assemble(held_grad[:KEPT], *back)
    return (query_grad, index_grad.reshape(blocks_here * BLOCK, feat_width))


def solution(mesh):
    wide, narrow = mesh.devices.shape
    split = Mesh(mesh.devices.reshape(wide // 2, 2, 4, narrow // 4), ("y", "c", "z", "x"))
    every = ("y", "c", "z", "x")
    group = ("y", "c")
    in_specs = (
        P(every, None),
        P(every, None),
        P(group),
        P(group),
        P(group),
        P(group, None),
        P(every, None),
        P(every),
    )
    out_specs = (P(every, None), P(every, None))
    return jax.shard_map(shard_work, mesh=split, in_specs=in_specs, out_specs=out_specs, check_vma=False)
```

```python
import functools
import math

import jax
import jax.numpy as jnp
from jax import lax
from jax.experimental import pallas as pl
from jax.experimental.pallas import tpu as pltpu
from jax.sharding import Mesh
from jax.sharding import PartitionSpec as P


BLOCK = 128
QTILE = 128
CAP = 2
SAME_CORE = ("y", "z", "x")
NARROW = ("z", "x")
KEPT = 16
SLAB = 8
STEPS = (("x", 1), ("x", -1), ("y", 1), ("y", -1), ("z", 1), ("z", -1))
PLACES = 2 * CAP * (1 + len(STEPS))
FIELDS = 6
COUNT_AT = PLACES * FIELDS
DEAD = -1e30
UNROLL = 12
VMEM_LIMIT = 60 * 1024 * 1024


def tile_bits(flags):
    places = jnp.arange(flags.shape[0], dtype=jnp.int32)[:, None]
    return jnp.sum(jnp.left_shift(flags.astype(jnp.int32), places), axis=0)


def ask_kernel(sizes, where, owner, local, hits, lives, table):
    ring, narrow_count, blocks_here = sizes
    ring_bits, narrow_bits = ring.bit_length() - 1, narrow_count.bit_length() - 1
    slab_bits = SLAB.bit_length() - 1
    first_slot, core = where[0], where[1]

    def clear(d, carry):
        table[d, COUNT_AT] = 0
        return carry

    lax.fori_loop(0, table.shape[0], clear, 0, unroll=8)

    def ask(j, carry):
        own, block = owner[j], local[j]
        wide = own >> narrow_bits
        narrow = own & (narrow_count - 1)
        turn = (block - KEPT) >> slab_bits
        spot = {"y": wide >> 1, "z": narrow >> ring_bits, "x": narrow & (ring - 1)}
        for k, (axis, shift) in enumerate(STEPS):
            spot[axis] = spot[axis] + jnp.where(turn == k, shift + ring, 0)
        edge = ring - 1
        dest = ((spot["y"] & edge) << (2 * ring_bits)) | ((spot["z"] & edge) << ring_bits) | (spot["x"] & edge)
        place = table[dest, COUNT_AT]
        table[dest, COUNT_AT] = place + 1
        at = place * FIELDS
        table[dest, at] = jnp.where((wide & 1) == core, 0, blocks_here) + block
        table[dest, at + 1] = first_slot + j
        table[dest, at + 2] = hits[j] & 0xFFFF
        table[dest, at + 3] = (hits[j] >> 16) & 0xFFFF
        table[dest, at + 4] = lives[j] & 0xFFFF
        table[dest, at + 5] = (lives[j] >> 16) & 0xFFFF
        return carry

    lax.fori_loop(0, owner.shape[0], ask, 0, unroll=4)


def list_kernel(table, first_items, second_items, counts, base, hits, live):
    groups = 4
    sources = table.shape[0]
    in_group = sources // groups
    dead = jnp.int32(sources)
    lists = (first_items, second_items)

    def group_entries(group, cursor):
        begin = cursor[2]

        def source_entries(n, count):
            src = group * in_group + n

            def place_entry(place, count):
                at = place * FIELDS
                base[count] = table[src, at] | (table[src, at + 1] << 7)
                hits[count] = table[src, at + 2] | (table[src, at + 3] << 16)
                live[count] = table[src, at + 4] | (table[src, at + 5] << 16)
                return count + 1

            return lax.fori_loop(0, table[src, COUNT_AT], place_entry, count)

        finish = lax.fori_loop(0, in_group, source_entries, begin)

        def entry_items(e, ends):
            start = (e << 7) + group * in_group
            alive = live[e]
            empty = (e << 7) + dead
            out = []
            for h, at in enumerate(ends):
                for n in range(in_group):
                    lists[h][at] = start + n
                    at = at + ((alive >> (2 * n + h)) & 1)
                lists[h][at] = empty
                out.append(at + (at & 1))
            return tuple(out)

        ends = lax.fori_loop(begin, finish, entry_items, cursor[:2])
        return ends + (finish,)

    zero = jnp.int32(0)
    base[0] = zero
    hits[0] = zero
    ends = lax.fori_loop(0, groups, group_entries, (zero, zero, zero))
    for h in range(2):
        for i in range(4 * UNROLL):
            lists[h][ends[h] + i] = dead
        counts[h] = (ends[h] + 2 * UNROLL - 1) // (2 * UNROLL)


def chunk_kernel(h, last, items, counts, base, hits, rows_in, q_in, own_in, mate_in, *rest):
    if last:
        earlier_in, query_out, own_out, mate_out, earlier, mate_acc = rest[:6]
    else:
        query_out, block_out = rest[:2]
    rows, q, blocks, query_acc, block_acc, scores, sems = rest[-7:]
    scale = 2.0 / math.sqrt(q.shape[2])
    factor = scale * math.log2(math.e)
    tiles = q_in.shape[0]
    here = own_in.shape[0]
    loads = [
        pltpu.make_async_copy(q_in, q.at[pl.ds(0, tiles)], sems.at[0]),
        pltpu.make_async_copy(own_in, blocks.at[pl.ds(0, here)], sems.at[1]),
        pltpu.make_async_copy(mate_in, blocks.at[pl.ds(here, here)], sems.at[2]),
        pltpu.make_async_copy(rows_in, rows.at[pl.ds(0, tiles)], sems.at[3]),
    ]
    if last:
        summed = pltpu.make_async_copy(earlier_in, earlier, sems.at[4])
    for load in loads:
        load.start()
    if last:
        summed.start()
    zero = jnp.zeros((BLOCK, QTILE), jnp.float32)
    q[tiles] = zero.astype(q.dtype)
    rows[tiles] = jnp.full(rows.shape[1:], -1.0, jnp.float32)
    query_acc[tiles] = zero

    def clear_query(t, carry):
        query_acc[t] = zero
        return carry

    def clear_block(b, carry):
        block_acc[b] = zero
        return carry

    lax.fori_loop(0, tiles, clear_query, 0, unroll=4)
    lax.fori_loop(0, 2 * here, clear_block, 0, unroll=4)
    scores[...] = jnp.zeros_like(scores)
    for load in loads:
        load.wait()

    column = lax.broadcasted_iota(jnp.int32, (BLOCK, QTILE), 0)

    def tile_of(word):
        return word & 127

    def block_of(word):
        return base[word >> 7] & 127

    def block_grads(words, grad):
        block = block_of(words[0])
        t1, t2 = tile_of(words[0]), tile_of(words[1])
        both = jnp.concatenate([q[t1], q[t2]], axis=0)
        to_block = jnp.dot(grad, both, preferred_element_type=jnp.float32)
        part = lax.dot_general(
            blocks[block], grad, (((0,), (0,)), ((), ())), preferred_element_type=jnp.float32
        )
        block_acc[block] += to_block
        sum1 = query_acc[t1] + part[:, :QTILE]
        sum2 = query_acc[t2] + part[:, QTILE:]
        query_acc[t1] = sum1
        query_acc[t2] = sum2

    def logit_grads(words, scores):
        slot = base[words[0] >> 7] >> 7
        halves = []
        for side, word in enumerate(words):
            tile = tile_of(word)
            hit = (hits[word >> 7] >> (2 * (tile & (tiles // 4 - 1)) + h)) & 1
            shift = rows[tile, pl.ds(h, 1), :]
            loss = rows[tile, pl.ds(2 + h, 1), :]
            positive = rows[tile, pl.ds(4 + h, 1), :].astype(jnp.int32)
            mine = (positive >> 7) == slot
            shift = jnp.where(jnp.logical_or(mine, hit > 0), shift, DEAD)
            target = jnp.where(mine, positive & 127, -1)
            at = slice(side * QTILE, (side + 1) * QTILE)
            terms = jnp.exp2(scores[:, at] * factor + shift)
            terms = terms - jnp.where(column == target, loss, 0.0)
            halves.append(terms.astype(jnp.bfloat16))
        return jnp.concatenate(halves, axis=1)

    def next_scores(words):
        both = jnp.concatenate([q[tile_of(words[0])], q[tile_of(words[1])]], axis=0)
        return lax.dot_general(
            blocks[block_of(words[0])], both, (((1,), (1,)), ((), ())), preferred_element_type=jnp.float32
        )

    def step(i, coming):
        starting = tuple((items[2 * (UNROLL * i + u)], items[2 * (UNROLL * i + u) + 1]) for u in range(UNROLL))
        for u in range(UNROLL):
            grad = logit_grads(coming[u], scores[u])
            block_grads(coming[u], grad)
            scores[u] = next_scores(starting[u])
        return starting

    dead = jnp.int32(tiles)
    lax.fori_loop(0, counts[h] + 1, step, ((dead, dead),) * UNROLL)

    if last:
        summed.wait()

        def deliver(b, carry):
            block_acc[b] = (block_acc[b] + earlier[b]) * scale
            mate_acc[b] = ((block_acc[b + here] + earlier[b + here]) * scale).astype(jnp.bfloat16)
            return carry

        lax.fori_loop(0, here, deliver, 0, unroll=2)
        stores = [
            pltpu.make_async_copy(mate_acc, mate_out, sems.at[5]),
            pltpu.make_async_copy(block_acc.at[pl.ds(0, here)], own_out, sems.at[6]),
        ]
    else:
        stores = [pltpu.make_async_copy(block_acc, block_out, sems.at[5])]
    for store in stores:
        store.start()

    def finish(t, carry):
        query_out[t] = (query_acc[t] * scale).T.astype(jnp.bfloat16)
        return carry

    lax.fori_loop(0, tiles, finish, 0, unroll=4)
    for store in stores:
        store.wait()


def hold_kernel(counts, kept, *rest):
    *lent, out = rest

    @pl.when(counts[0] >= 0)
    def _():
        out[pl.ds(0, KEPT)] = kept[...]
        for k, part in enumerate(lent):
            out[pl.ds(KEPT + SLAB * k, SLAB)] = part[...]


def assemble_kernel(kept, *rest):
    *back, out = rest
    out[pl.ds(0, KEPT)] = kept[...]
    for k, part in enumerate(back):
        out[pl.ds(KEPT + SLAB * k, SLAB)] = part[...].astype(jnp.float32)


def shard_work(
    queries, index_rows, lse_shift, loss_weight, positives, tile_negs, fetch_owner, fetch_local
):
    narrow_count = lax.axis_size(NARROW)
    sources = lax.axis_size(SAME_CORE)
    core = lax.axis_index("c")
    narrow_pos = lax.axis_index(NARROW)
    feat_width = queries.shape[1]
    own_rows = queries.shape[0]
    blocks_here = index_rows.shape[0] // BLOCK
    stored = index_rows.reshape(blocks_here, BLOCK, feat_width)
    halves = []
    for h in range(2):
        part = queries[h * QTILE : (h + 1) * QTILE]
        spread = jnp.broadcast_to(part[None], (sources, QTILE, feat_width))
        halves.append(lax.all_to_all(spread, SAME_CORE, 0, 0, tiled=True))
    ring = lax.axis_size("x")
    ways = []
    for axis, shift in STEPS:
        size = lax.axis_size(axis)
        ways.append((axis, [(i, (i + shift) % size) for i in range(size)]))
    slabs = [slice(KEPT + SLAB * k, KEPT + SLAB * (k + 1)) for k in range(len(STEPS))]
    lent = [lax.ppermute(stored[at], axis, way) for at, (axis, way) in zip(slabs, ways)]
    kept = stored[:KEPT]
    smem = pl.BlockSpec(memory_space=pltpu.SMEM)
    vmem = pl.BlockSpec(memory_space=pltpu.VMEM)
    limit = pltpu.CompilerParams(vmem_limit_bytes=VMEM_LIMIT)
    owners = fetch_owner[:, 0]
    fetch_count = owners.shape[0]
    first_slot = narrow_pos * fetch_count
    slot_ids = first_slot + jnp.arange(fetch_count, dtype=jnp.int32)
    tile_hit = jnp.any(tile_negs[:, :, None] == slot_ids[None, None, :], axis=1)
    tiles = tile_negs.shape[0]
    pos_slots = positives.reshape(tiles, QTILE) // BLOCK
    pos_hit = jnp.any(pos_slots[:, :, None] == slot_ids[None, None, :], axis=1)
    ask = pl.pallas_call(
        functools.partial(ask_kernel, (ring, narrow_count, blocks_here)),
        out_shape=jax.ShapeDtypeStruct((sources, 2 * QTILE), jnp.int32),
        in_specs=[smem] * 5,
        out_specs=smem,
        cost_estimate=pl.CostEstimate(flops=10**6, bytes_accessed=2**16, transcendentals=0),
        name="ask",
    )
    table = ask(
        jnp.stack([first_slot, core]),
        owners,
        fetch_local,
        tile_bits(tile_hit),
        tile_bits(jnp.logical_or(tile_hit, pos_hit)),
    )
    first_row = narrow_pos * own_rows
    lse_own = lax.dynamic_slice_in_dim(lse_shift, first_row, own_rows, 0)
    loss_own = lax.dynamic_slice_in_dim(loss_weight, first_row, own_rows, 0)
    pos_own = lax.dynamic_slice_in_dim(positives, first_row, own_rows, 0)
    lse_full = lse_own + math.log(fetch_count * narrow_count * BLOCK)
    shift = jnp.log2(loss_own) - lse_full * math.log2(math.e)
    per_query = jnp.concatenate([shift, loss_own, pos_own.astype(jnp.float32)]).reshape(6, QTILE)
    per_query = jnp.broadcast_to(per_query[None], (sources, 6, QTILE))
    packed = table.astype(jnp.float32).reshape(sources, 2, QTILE)
    packed = jnp.concatenate([per_query, packed], axis=1)
    rows = lax.all_to_all(packed, SAME_CORE, 0, 0, tiled=True)
    table = rows[:, 6:].astype(jnp.int32).reshape(sources, 2 * QTILE)
    most = sources * PLACES * (tiles // 2) + 4 * UNROLL
    list_shape = jax.ShapeDtypeStruct((most,), jnp.int32)
    entry_shape = jax.ShapeDtypeStruct((sources * PLACES,), jnp.int32)
    listing = pl.pallas_call(
        list_kernel,
        out_shape=(list_shape, list_shape, jax.ShapeDtypeStruct((2,), jnp.int32), entry_shape, entry_shape),
        in_specs=[smem],
        out_specs=(smem,) * 5,
        scratch_shapes=[pltpu.SMEM(entry_shape.shape, jnp.int32)],
        cost_estimate=pl.CostEstimate(flops=10**9, bytes_accessed=2**20, transcendentals=0),
        name="listing",
    )
    *items, counts, base, hits = listing(table)
    hold = pl.pallas_call(
        hold_kernel,
        out_shape=jax.ShapeDtypeStruct(stored.shape, stored.dtype),
        in_specs=[smem] + [vmem] * (1 + len(lent)),
        out_specs=vmem,
        compiler_params=limit,
        cost_estimate=pl.CostEstimate(flops=10**6, bytes_accessed=2**22, transcendentals=0),
        name="hold",
    )
    held = hold(counts, kept, *lent)
    mate_held = lax.ppermute(held, "c", [(0, 1), (1, 0)])

    acc_shape = jax.ShapeDtypeStruct((2 * blocks_here, BLOCK, feat_width), jnp.float32)
    grad_shape = jax.ShapeDtypeStruct((sources, QTILE, feat_width), jnp.bfloat16)
    own_shape = jax.ShapeDtypeStruct((blocks_here, BLOCK, feat_width), jnp.float32)
    mate_shape = jax.ShapeDtypeStruct((blocks_here, BLOCK, feat_width), jnp.bfloat16)

    def scratch(extra):
        return extra + [
            pltpu.VMEM((sources + 1, 8, QTILE), jnp.float32),
            pltpu.VMEM((sources + 1, QTILE, feat_width), jnp.bfloat16),
            pltpu.VMEM((2 * blocks_here, BLOCK, feat_width), jnp.bfloat16),
            pltpu.VMEM((sources + 1, feat_width, QTILE), jnp.float32),
            pltpu.VMEM(acc_shape.shape, jnp.float32),
            pltpu.VMEM((UNROLL, BLOCK, 2 * QTILE), jnp.float32),
            pltpu.SemaphoreType.DMA((7,)),
        ]

    hbm = pl.BlockSpec(memory_space=pl.ANY)
    cost = pl.CostEstimate(flops=2 * 10**10, bytes_accessed=2**25, transcendentals=10**7)
    chunk_0 = pl.pallas_call(
        functools.partial(chunk_kernel, 0, False),
        out_shape=(grad_shape, acc_shape),
        in_specs=[smem] * 4 + [hbm] * 4,
        out_specs=(vmem, hbm),
        scratch_shapes=scratch([]),
        compiler_params=limit,
        cost_estimate=cost,
        name="chunk_0",
    )
    grad_0, acc = chunk_0(items[0], counts, base, hits, rows, halves[0], held, mate_held)
    chunk_1 = pl.pallas_call(
        functools.partial(chunk_kernel, 1, True),
        out_shape=(grad_shape, own_shape, mate_shape),
        in_specs=[smem] * 4 + [hbm] * 5,
        out_specs=(vmem, hbm, hbm),
        scratch_shapes=scratch(
            [pltpu.VMEM(acc_shape.shape, jnp.float32), pltpu.VMEM(mate_shape.shape, jnp.bfloat16)]
        ),
        compiler_params=limit,
        cost_estimate=cost,
        name="chunk_1",
    )
    grad_1, own_grad, mate_grad = chunk_1(items[1], counts, base, hits, rows, halves[1], held, mate_held, acc)
    sums = []
    for part in (grad_0, grad_1):
        came = lax.all_to_all(part, SAME_CORE, 0, 0, tiled=True)
        sums.append(jnp.sum(came.astype(jnp.float32), axis=0))
    query_grad = jnp.concatenate(sums)
    from_mate = lax.ppermute(mate_grad, "c", [(0, 1), (1, 0)])
    held_grad = own_grad + from_mate.astype(jnp.float32)
    back = [
        lax.ppermute(held_grad[at].astype(jnp.bfloat16), axis, [(j, i) for i, j in way])
        for at, (axis, way) in zip(slabs, ways)
    ]
    assemble = pl.pallas_call(
        assemble_kernel,
        out_shape=own_shape,
        in_specs=[vmem] * (1 + len(back)),
        out_specs=vmem,
        compiler_params=limit,
        cost_estimate=pl.CostEstimate(flops=10**6, bytes_accessed=2**23, transcendentals=0),
        name="assemble",
    )
    index_grad = assemble(held_grad[:KEPT], *back)
    return (query_grad, index_grad.reshape(blocks_here * BLOCK, feat_width))


def solution(mesh):
    wide, narrow = mesh.devices.shape
    split = Mesh(mesh.devices.reshape(wide // 2, 2, 4, narrow // 4), ("y", "c", "z", "x"))
    every = ("y", "c", "z", "x")
    group = ("y", "c")
    in_specs = (
        P(every, None),
        P(every, None),
        P(group),
        P(group),
        P(group),
        P(group, None),
        P(every, None),
        P(every),
    )
    out_specs = (P(every, None), P(every, None))
    return jax.shard_map(shard_work, mesh=split, in_specs=in_specs, out_specs=out_specs, check_vma=False)
```

```python
import functools
import math

import jax
import jax.numpy as jnp
from jax import lax
from jax.experimental import pallas as pl
from jax.experimental.pallas import tpu as pltpu
from jax.sharding import Mesh
from jax.sharding import PartitionSpec as P


BLOCK = 128
QTILE = 128
CAP = 2
SAME_CORE = ("y", "z", "x")
NARROW = ("z", "x")
KEPT = 16
SLAB = 8
STEPS = (("x", 1), ("x", -1), ("y", 1), ("y", -1), ("z", 1), ("z", -1))
PLACES = 2 * CAP * (1 + len(STEPS))
FIELDS = 6
COUNT_AT = PLACES * FIELDS
DEAD = -1e30
UNROLL = 12
PIECE = 2048
VMEM_LIMIT = 60 * 1024 * 1024


def tile_bits(flags):
    places = jnp.arange(flags.shape[0], dtype=jnp.int32)[:, None]
    return jnp.sum(jnp.left_shift(flags.astype(jnp.int32), places), axis=0)


def ask_kernel(sizes, where, owner, local, hits, lives, table):
    ring, narrow_count, blocks_here = sizes
    ring_bits, narrow_bits = ring.bit_length() - 1, narrow_count.bit_length() - 1
    slab_bits = SLAB.bit_length() - 1
    first_slot, core = where[0], where[1]

    def clear(d, carry):
        table[d, COUNT_AT] = 0
        return carry

    lax.fori_loop(0, table.shape[0], clear, 0, unroll=8)

    def ask(j, carry):
        own, block = owner[j], local[j]
        wide = own >> narrow_bits
        narrow = own & (narrow_count - 1)
        turn = (block - KEPT) >> slab_bits
        spot = {"y": wide >> 1, "z": narrow >> ring_bits, "x": narrow & (ring - 1)}
        for k, (axis, shift) in enumerate(STEPS):
            spot[axis] = spot[axis] + jnp.where(turn == k, shift + ring, 0)
        edge = ring - 1
        dest = ((spot["y"] & edge) << (2 * ring_bits)) | ((spot["z"] & edge) << ring_bits) | (spot["x"] & edge)
        place = table[dest, COUNT_AT]
        table[dest, COUNT_AT] = place + 1
        at = place * FIELDS
        table[dest, at] = jnp.where((wide & 1) == core, 0, blocks_here) + block
        table[dest, at + 1] = first_slot + j
        table[dest, at + 2] = hits[j] & 0xFFFF
        table[dest, at + 3] = (hits[j] >> 16) & 0xFFFF
        table[dest, at + 4] = lives[j] & 0xFFFF
        table[dest, at + 5] = (lives[j] >> 16) & 0xFFFF
        return carry

    lax.fori_loop(0, owner.shape[0], ask, 0, unroll=4)


def list_kernel(table, first_items, second_items, counts, base, hits, live):
    groups = 4
    sources = table.shape[0]
    in_group = sources // groups
    dead = jnp.int32(sources)
    lists = (first_items, second_items)

    def group_entries(group, cursor):
        begin = cursor[2]

        def source_entries(n, count):
            src = group * in_group + n

            def place_entry(place, count):
                at = place * FIELDS
                base[count] = table[src, at] | (table[src, at + 1] << 7)
                hits[count] = table[src, at + 2] | (table[src, at + 3] << 16)
                live[count] = table[src, at + 4] | (table[src, at + 5] << 16)
                return count + 1

            return lax.fori_loop(0, table[src, COUNT_AT], place_entry, count)

        finish = lax.fori_loop(0, in_group, source_entries, begin)

        def entry_items(e, ends):
            start = (e << 7) + group * in_group
            alive = live[e]
            empty = (e << 7) + dead
            out = []
            for h, at in enumerate(ends):
                for n in range(in_group):
                    lists[h][at] = start + n
                    at = at + ((alive >> (2 * n + h)) & 1)
                lists[h][at] = empty
                out.append(at + (at & 1))
            return tuple(out)

        ends = lax.fori_loop(begin, finish, entry_items, cursor[:2])
        return ends + (finish,)

    zero = jnp.int32(0)
    base[0] = zero
    hits[0] = zero
    ends = lax.fori_loop(0, groups, group_entries, (zero, zero, zero))
    for h in range(2):
        for i in range(4 * UNROLL):
            lists[h][ends[h] + i] = dead
        counts[h] = (ends[h] + 2 * UNROLL - 1) // (2 * UNROLL)


def chunk_kernel(h, last, counts, base, hits, items_in, rows_in, q_in, own_in, mate_in, *rest):
    if last:
        earlier_in, query_out, own_out, mate_out, earlier, mate_acc = rest[:6]
    else:
        query_out, block_out = rest[:2]
    items, rows, q, blocks, query_acc, block_acc, scores, sems = rest[-8:]
    scale = 2.0 / math.sqrt(q.shape[2])
    factor = scale * math.log2(math.e)
    tiles = q_in.shape[0]
    here = own_in.shape[0]
    loads = [
        pltpu.make_async_copy(q_in, q.at[pl.ds(0, tiles)], sems.at[0]),
        pltpu.make_async_copy(own_in, blocks.at[pl.ds(0, here)], sems.at[1]),
        pltpu.make_async_copy(mate_in, blocks.at[pl.ds(here, here)], sems.at[2]),
        pltpu.make_async_copy(rows_in, rows.at[pl.ds(0, tiles)], sems.at[3]),
    ]
    if last:
        summed = pltpu.make_async_copy(earlier_in, earlier, sems.at[4])
    for load in loads:
        load.start()
    if last:
        summed.start()

    def load_items(i, carry):
        at = pl.ds(pl.multiple_of(i * PIECE, PIECE), PIECE)
        piece = pltpu.make_async_copy(items_in.at[at], items.at[at], sems.at[7])
        piece.start()
        piece.wait()
        return carry

    lax.fori_loop(0, (2 * UNROLL * (counts[h] + 1) + PIECE - 1) // PIECE, load_items, 0)
    zero = jnp.zeros((BLOCK, QTILE), jnp.float32)
    q[tiles] = zero.astype(q.dtype)
    rows[tiles] = jnp.full(rows.shape[1:], -1.0, jnp.float32)
    query_acc[tiles] = zero

    def clear_query(t, carry):
        query_acc[t] = zero
        return carry

    def clear_block(b, carry):
        block_acc[b] = zero
        return carry

    lax.fori_loop(0, tiles, clear_query, 0, unroll=4)
    lax.fori_loop(0, 2 * here, clear_block, 0, unroll=4)
    scores[...] = jnp.zeros_like(scores)
    for load in loads:
        load.wait()

    column = lax.broadcasted_iota(jnp.int32, (BLOCK, QTILE), 0)

    def tile_of(word):
        return word & 127

    def block_of(word):
        return base[word >> 7] & 127

    def block_grads(words, grad):
        block = block_of(words[0])
        t1, t2 = tile_of(words[0]), tile_of(words[1])
        both = jnp.concatenate([q[t1], q[t2]], axis=0)
        to_block = jnp.dot(grad, both, preferred_element_type=jnp.float32)
        part = lax.dot_general(
            blocks[block], grad, (((0,), (0,)), ((), ())), preferred_element_type=jnp.float32
        )
        block_acc[block] += to_block
        sum1 = query_acc[t1] + part[:, :QTILE]
        sum2 = query_acc[t2] + part[:, QTILE:]
        query_acc[t1] = sum1
        query_acc[t2] = sum2

    def logit_grads(words, scores):
        slot = base[words[0] >> 7] >> 7
        halves = []
        for side, word in enumerate(words):
            tile = tile_of(word)
            hit = (hits[word >> 7] >> (2 * (tile & (tiles // 4 - 1)) + h)) & 1
            shift = rows[tile, pl.ds(h, 1), :]
            loss = rows[tile, pl.ds(2 + h, 1), :]
            positive = rows[tile, pl.ds(4 + h, 1), :].astype(jnp.int32)
            mine = (positive >> 7) == slot
            shift = jnp.where(jnp.logical_or(mine, hit > 0), shift, DEAD)
            target = jnp.where(mine, positive & 127, -1)
            at = slice(side * QTILE, (side + 1) * QTILE)
            terms = jnp.exp2(scores[:, at] * factor + shift)
            terms = terms - jnp.where(column == target, loss, 0.0)
            halves.append(terms.astype(jnp.bfloat16))
        return jnp.concatenate(halves, axis=1)

    def next_scores(words):
        both = jnp.concatenate([q[tile_of(words[0])], q[tile_of(words[1])]], axis=0)
        return lax.dot_general(
            blocks[block_of(words[0])], both, (((1,), (1,)), ((), ())), preferred_element_type=jnp.float32
        )

    def step(i, coming):
        starting = tuple((items[2 * (UNROLL * i + u)], items[2 * (UNROLL * i + u) + 1]) for u in range(UNROLL))
        for u in range(UNROLL):
            grad = logit_grads(coming[u], scores[u])
            block_grads(coming[u], grad)
            scores[u] = next_scores(starting[u])
        return starting

    dead = jnp.int32(tiles)
    lax.fori_loop(0, counts[h] + 1, step, ((dead, dead),) * UNROLL)

    if last:
        summed.wait()

        def deliver(b, carry):
            block_acc[b] = (block_acc[b] + earlier[b]) * scale
            mate_acc[b] = ((block_acc[b + here] + earlier[b + here]) * scale).astype(jnp.bfloat16)
            return carry

        lax.fori_loop(0, here, deliver, 0, unroll=2)
        stores = [
            pltpu.make_async_copy(mate_acc, mate_out, sems.at[5]),
            pltpu.make_async_copy(block_acc.at[pl.ds(0, here)], own_out, sems.at[6]),
        ]
    else:
        stores = [pltpu.make_async_copy(block_acc, block_out, sems.at[5])]
    for store in stores:
        store.start()

    def finish(t, carry):
        query_out[t] = (query_acc[t] * scale).T.astype(jnp.bfloat16)
        return carry

    lax.fori_loop(0, tiles, finish, 0, unroll=4)
    for store in stores:
        store.wait()


def hold_kernel(kept, *rest):
    *lent, out = rest
    out[pl.ds(0, KEPT)] = kept[...]
    for k, part in enumerate(lent):
        out[pl.ds(KEPT + SLAB * k, SLAB)] = part[...]


def assemble_kernel(kept, *rest):
    *back, out = rest
    out[pl.ds(0, KEPT)] = kept[...]
    for k, part in enumerate(back):
        out[pl.ds(KEPT + SLAB * k, SLAB)] = part[...].astype(jnp.float32)


def shard_work(
    queries, index_rows, lse_shift, loss_weight, positives, tile_negs, fetch_owner, fetch_local
):
    narrow_count = lax.axis_size(NARROW)
    sources = lax.axis_size(SAME_CORE)
    core = lax.axis_index("c")
    narrow_pos = lax.axis_index(NARROW)
    feat_width = queries.shape[1]
    own_rows = queries.shape[0]
    blocks_here = index_rows.shape[0] // BLOCK
    stored = index_rows.reshape(blocks_here, BLOCK, feat_width)
    halves = []
    for h in range(2):
        part = queries[h * QTILE : (h + 1) * QTILE]
        spread = jnp.broadcast_to(part[None], (sources, QTILE, feat_width))
        halves.append(lax.all_to_all(spread, SAME_CORE, 0, 0, tiled=True))
    ring = lax.axis_size("x")
    ways = []
    for axis, shift in STEPS:
        size = lax.axis_size(axis)
        ways.append((axis, [(i, (i + shift) % size) for i in range(size)]))
    slabs = [slice(KEPT + SLAB * k, KEPT + SLAB * (k + 1)) for k in range(len(STEPS))]
    lent = [lax.ppermute(stored[at], axis, way) for at, (axis, way) in zip(slabs, ways)]
    kept = stored[:KEPT]
    smem = pl.BlockSpec(memory_space=pltpu.SMEM)
    vmem = pl.BlockSpec(memory_space=pltpu.VMEM)
    limit = pltpu.CompilerParams(vmem_limit_bytes=VMEM_LIMIT)
    owners = fetch_owner[:, 0]
    fetch_count = owners.shape[0]
    first_slot = narrow_pos * fetch_count
    slot_ids = first_slot + jnp.arange(fetch_count, dtype=jnp.int32)
    tile_hit = jnp.any(tile_negs[:, :, None] == slot_ids[None, None, :], axis=1)
    tiles = tile_negs.shape[0]
    pos_slots = positives.reshape(tiles, QTILE) // BLOCK
    pos_hit = jnp.any(pos_slots[:, :, None] == slot_ids[None, None, :], axis=1)
    ask = pl.pallas_call(
        functools.partial(ask_kernel, (ring, narrow_count, blocks_here)),
        out_shape=jax.ShapeDtypeStruct((sources, 2 * QTILE), jnp.int32),
        in_specs=[smem] * 5,
        out_specs=smem,
        cost_estimate=pl.CostEstimate(flops=10**6, bytes_accessed=2**16, transcendentals=0),
        name="ask",
    )
    hits = tile_bits(tile_hit)
    lives = tile_bits(jnp.logical_or(tile_hit, pos_hit))
    table = ask(jnp.stack([first_slot, core]), owners, fetch_local, hits, lives)
    first_row = narrow_pos * own_rows
    lse_own = lax.dynamic_slice_in_dim(lse_shift, first_row, own_rows, 0)
    loss_own = lax.dynamic_slice_in_dim(loss_weight, first_row, own_rows, 0)
    pos_own = lax.dynamic_slice_in_dim(positives, first_row, own_rows, 0)
    lse_full = lse_own + math.log(fetch_count * narrow_count * BLOCK)
    shift = jnp.log2(loss_own) - lse_full * math.log2(math.e)
    per_query = jnp.concatenate([shift, loss_own, pos_own.astype(jnp.float32)]).reshape(6, QTILE)
    per_query = jnp.broadcast_to(per_query[None], (sources, 6, QTILE))
    packed = table.astype(jnp.float32).reshape(sources, 2, QTILE)
    packed = jnp.concatenate([per_query, packed], axis=1)
    rows = lax.all_to_all(packed, SAME_CORE, 0, 0, tiled=True)
    table = rows[:, 6:].astype(jnp.int32).reshape(sources, 2 * QTILE)
    most = -(-(sources * PLACES * (tiles // 2) + 4 * UNROLL) // PIECE) * PIECE
    list_shape = jax.ShapeDtypeStruct((most,), jnp.int32)
    entry_shape = jax.ShapeDtypeStruct((sources * PLACES,), jnp.int32)
    listing = pl.pallas_call(
        list_kernel,
        out_shape=(list_shape, list_shape, jax.ShapeDtypeStruct((2,), jnp.int32), entry_shape, entry_shape),
        in_specs=[smem],
        out_specs=(smem,) * 5,
        scratch_shapes=[pltpu.SMEM(entry_shape.shape, jnp.int32)],
        cost_estimate=pl.CostEstimate(flops=10**9, bytes_accessed=2**20, transcendentals=0),
        name="listing",
    )
    *items, counts, base, hits = listing(table)
    hold = pl.pallas_call(
        hold_kernel,
        out_shape=jax.ShapeDtypeStruct(stored.shape, stored.dtype),
        in_specs=[vmem] * (1 + len(lent)),
        out_specs=vmem,
        compiler_params=limit,
        cost_estimate=pl.CostEstimate(flops=10**6, bytes_accessed=2**22, transcendentals=0),
        name="hold",
    )
    held = hold(kept, *lent)
    mate_held = lax.ppermute(held, "c", [(0, 1), (1, 0)])

    acc_shape = jax.ShapeDtypeStruct((2 * blocks_here, BLOCK, feat_width), jnp.float32)
    grad_shape = jax.ShapeDtypeStruct((sources, QTILE, feat_width), jnp.bfloat16)
    own_shape = jax.ShapeDtypeStruct((blocks_here, BLOCK, feat_width), jnp.float32)
    mate_shape = jax.ShapeDtypeStruct((blocks_here, BLOCK, feat_width), jnp.bfloat16)

    def scratch(extra):
        return extra + [
            pltpu.SMEM((most,), jnp.int32),
            pltpu.VMEM((sources + 1, 8, QTILE), jnp.float32),
            pltpu.VMEM((sources + 1, QTILE, feat_width), jnp.bfloat16),
            pltpu.VMEM((2 * blocks_here, BLOCK, feat_width), jnp.bfloat16),
            pltpu.VMEM((sources + 1, feat_width, QTILE), jnp.float32),
            pltpu.VMEM(acc_shape.shape, jnp.float32),
            pltpu.VMEM((UNROLL, BLOCK, 2 * QTILE), jnp.float32),
            pltpu.SemaphoreType.DMA((8,)),
        ]

    hbm = pl.BlockSpec(memory_space=pl.ANY)
    cost = pl.CostEstimate(flops=2 * 10**10, bytes_accessed=2**25, transcendentals=10**7)
    chunk_0 = pl.pallas_call(
        functools.partial(chunk_kernel, 0, False),
        out_shape=(grad_shape, acc_shape),
        in_specs=[smem] * 3 + [hbm] * 5,
        out_specs=(vmem, hbm),
        scratch_shapes=scratch([]),
        compiler_params=limit,
        cost_estimate=cost,
        name="chunk_0",
    )
    grad_0, acc = chunk_0(counts, base, hits, items[0], rows, halves[0], held, mate_held)
    chunk_1 = pl.pallas_call(
        functools.partial(chunk_kernel, 1, True),
        out_shape=(grad_shape, own_shape, mate_shape),
        in_specs=[smem] * 3 + [hbm] * 6,
        out_specs=(vmem, hbm, hbm),
        scratch_shapes=scratch(
            [pltpu.VMEM(acc_shape.shape, jnp.float32), pltpu.VMEM(mate_shape.shape, jnp.bfloat16)]
        ),
        compiler_params=limit,
        cost_estimate=cost,
        name="chunk_1",
    )
    grad_1, own_grad, mate_grad = chunk_1(counts, base, hits, items[1], rows, halves[1], held, mate_held, acc)
    sums = []
    for part in (grad_0, grad_1):
        came = lax.all_to_all(part, SAME_CORE, 0, 0, tiled=True)
        sums.append(jnp.sum(came.astype(jnp.float32), axis=0))
    query_grad = jnp.concatenate(sums)
    from_mate = lax.ppermute(mate_grad, "c", [(0, 1), (1, 0)])
    held_grad = own_grad + from_mate.astype(jnp.float32)
    back = [
        lax.ppermute(held_grad[at].astype(jnp.bfloat16), axis, [(j, i) for i, j in way])
        for at, (axis, way) in zip(slabs, ways)
    ]
    assemble = pl.pallas_call(
        assemble_kernel,
        out_shape=own_shape,
        in_specs=[vmem] * (1 + len(back)),
        out_specs=vmem,
        compiler_params=limit,
        cost_estimate=pl.CostEstimate(flops=10**6, bytes_accessed=2**23, transcendentals=0),
        name="assemble",
    )
    index_grad = assemble(held_grad[:KEPT], *back)
    return (query_grad, index_grad.reshape(blocks_here * BLOCK, feat_width))


def solution(mesh):
    wide, narrow = mesh.devices.shape
    split = Mesh(mesh.devices.reshape(wide // 2, 2, 4, narrow // 4), ("y", "c", "z", "x"))
    every = ("y", "c", "z", "x")
    group = ("y", "c")
    in_specs = (
        P(every, None),
        P(every, None),
        P(group),
        P(group),
        P(group),
        P(group, None),
        P(every, None),
        P(every),
    )
    out_specs = (P(every, None), P(every, None))
    return jax.shard_map(shard_work, mesh=split, in_specs=in_specs, out_specs=out_specs, check_vma=False)
```

```python
import functools
import math

import jax
import jax.numpy as jnp
from jax import lax
from jax.experimental import pallas as pl
from jax.experimental.pallas import tpu as pltpu
from jax.sharding import Mesh
from jax.sharding import PartitionSpec as P


BLOCK = 128
QTILE = 128
CAP = 2
SAME_CORE = ("y", "z", "x")
NARROW = ("z", "x")
KEPT = 16
SLAB = 8
STEPS = (("x", 1), ("x", -1), ("y", 1), ("y", -1), ("z", 1), ("z", -1))
PLACES = 2 * CAP * (1 + len(STEPS))
FIELDS = 6
COUNT_AT = PLACES * FIELDS
DEAD = -1e30
UNROLL = 12
PIECE = 2048
VMEM_LIMIT = 60 * 1024 * 1024


def tile_bits(flags):
    places = jnp.arange(flags.shape[0], dtype=jnp.int32)[:, None]
    return jnp.sum(jnp.left_shift(flags.astype(jnp.int32), places), axis=0)


def ask_kernel(sizes, where, owner, local, hits, lives, table):
    ring, narrow_count, blocks_here = sizes
    ring_bits, narrow_bits = ring.bit_length() - 1, narrow_count.bit_length() - 1
    slab_bits = SLAB.bit_length() - 1
    first_slot, core = where[0], where[1]

    def clear(d, carry):
        table[d, COUNT_AT] = 0
        return carry

    lax.fori_loop(0, table.shape[0], clear, 0, unroll=8)

    def ask(j, carry):
        own, block = owner[j], local[j]
        wide = own >> narrow_bits
        narrow = own & (narrow_count - 1)
        turn = (block - KEPT) >> slab_bits
        spot = {"y": wide >> 1, "z": narrow >> ring_bits, "x": narrow & (ring - 1)}
        for k, (axis, shift) in enumerate(STEPS):
            spot[axis] = spot[axis] + jnp.where(turn == k, shift + ring, 0)
        edge = ring - 1
        dest = ((spot["y"] & edge) << (2 * ring_bits)) | ((spot["z"] & edge) << ring_bits) | (spot["x"] & edge)
        place = table[dest, COUNT_AT]
        table[dest, COUNT_AT] = place + 1
        at = place * FIELDS
        table[dest, at] = jnp.where((wide & 1) == core, 0, blocks_here) + block
        table[dest, at + 1] = first_slot + j
        table[dest, at + 2] = hits[j] & 0xFFFF
        table[dest, at + 3] = (hits[j] >> 16) & 0xFFFF
        table[dest, at + 4] = lives[j] & 0xFFFF
        table[dest, at + 5] = (lives[j] >> 16) & 0xFFFF
        return carry

    lax.fori_loop(0, owner.shape[0], ask, 0, unroll=4)


def list_kernel(table, first_out, second_out, counts, base, hits, live, first_items, second_items, sems):
    groups = 4
    sources = table.shape[0]
    in_group = sources // groups
    dead = jnp.int32(sources)
    lists = (first_items, second_items)

    def group_entries(group, cursor):
        begin = cursor[2]

        def source_entries(n, count):
            src = group * in_group + n

            def place_entry(place, count):
                at = place * FIELDS
                base[count] = table[src, at] | (table[src, at + 1] << 7)
                hits[count] = table[src, at + 2] | (table[src, at + 3] << 16)
                live[count] = table[src, at + 4] | (table[src, at + 5] << 16)
                return count + 1

            return lax.fori_loop(0, table[src, COUNT_AT], place_entry, count)

        finish = lax.fori_loop(0, in_group, source_entries, begin)

        def entry_items(e, ends):
            start = (e << 7) + group * in_group
            alive = live[e]
            empty = (e << 7) + dead
            out = []
            for h, at in enumerate(ends):
                for n in range(in_group):
                    lists[h][at] = start + n
                    at = at + ((alive >> (2 * n + h)) & 1)
                lists[h][at] = empty
                out.append(at + (at & 1))
            return tuple(out)

        ends = lax.fori_loop(begin, finish, entry_items, cursor[:2])
        return ends + (finish,)

    zero = jnp.int32(0)
    base[0] = zero
    hits[0] = zero
    ends = lax.fori_loop(0, groups, group_entries, (zero, zero, zero))
    for h in range(2):
        for i in range(4 * UNROLL):
            lists[h][ends[h] + i] = dead
        count = (ends[h] + 2 * UNROLL - 1) // (2 * UNROLL)
        counts[h] = count
        target = (first_out, second_out)[h]

        def store_items(i, carry, h=h, target=target):
            at = pl.ds(pl.multiple_of(i * PIECE, PIECE), PIECE)
            piece = pltpu.make_async_copy(lists[h].at[at], target.at[at], sems.at[h])
            piece.start()
            piece.wait()
            return carry

        lax.fori_loop(0, (2 * UNROLL * (count + 1) + PIECE - 1) // PIECE, store_items, 0)


def chunk_kernel(h, last, counts, base, hits, items_in, rows_in, q_in, own_in, mate_in, *rest):
    if last:
        earlier_in, query_out, own_out, mate_out, earlier, mate_acc = rest[:6]
    else:
        query_out, block_out = rest[:2]
    items, rows, q, blocks, query_acc, block_acc, scores, query_grad, sems = rest[-9:]
    scale = 2.0 / math.sqrt(q.shape[2])
    factor = scale * math.log2(math.e)
    tiles = q_in.shape[0]
    here = own_in.shape[0]
    loads = [
        pltpu.make_async_copy(q_in, q.at[pl.ds(0, tiles)], sems.at[0]),
        pltpu.make_async_copy(own_in, blocks.at[pl.ds(0, here)], sems.at[1]),
        pltpu.make_async_copy(mate_in, blocks.at[pl.ds(here, here)], sems.at[2]),
        pltpu.make_async_copy(rows_in, rows.at[pl.ds(0, tiles)], sems.at[3]),
    ]
    if last:
        summed = pltpu.make_async_copy(earlier_in, earlier, sems.at[4])
    for load in loads:
        load.start()
    if last:
        summed.start()

    def load_items(i, carry):
        at = pl.ds(pl.multiple_of(i * PIECE, PIECE), PIECE)
        piece = pltpu.make_async_copy(items_in.at[at], items.at[at], sems.at[7])
        piece.start()
        piece.wait()
        return carry

    lax.fori_loop(0, (2 * UNROLL * (counts[h] + 1) + PIECE - 1) // PIECE, load_items, 0)
    zero = jnp.zeros((BLOCK, QTILE), jnp.float32)
    q[tiles] = zero.astype(q.dtype)
    rows[tiles] = jnp.full(rows.shape[1:], -1.0, jnp.float32)
    query_acc[tiles] = zero

    def clear_query(t, carry):
        query_acc[t] = zero
        return carry

    def clear_block(b, carry):
        block_acc[b] = zero
        return carry

    lax.fori_loop(0, tiles, clear_query, 0, unroll=4)
    lax.fori_loop(0, 2 * here, clear_block, 0, unroll=4)
    scores[...] = jnp.zeros_like(scores)
    for load in loads:
        load.wait()

    column = lax.broadcasted_iota(jnp.int32, (BLOCK, QTILE), 0)

    def tile_of(word):
        return word & 127

    def block_of(word):
        return base[word >> 7] & 127

    def block_grads(words, grad):
        block = block_of(words[0])
        t1, t2 = tile_of(words[0]), tile_of(words[1])
        both = jnp.concatenate([q[t1], q[t2]], axis=0)
        to_block = jnp.dot(grad, both, preferred_element_type=jnp.float32)
        part = lax.dot_general(
            blocks[block], grad, (((0,), (0,)), ((), ())), preferred_element_type=jnp.float32
        )
        block_acc[block] += to_block
        sum1 = query_acc[t1] + part[:, :QTILE]
        sum2 = query_acc[t2] + part[:, QTILE:]
        query_acc[t1] = sum1
        query_acc[t2] = sum2

    def logit_grads(words, scores):
        slot = base[words[0] >> 7] >> 7
        halves = []
        for side, word in enumerate(words):
            tile = tile_of(word)
            hit = (hits[word >> 7] >> (2 * (tile & (tiles // 4 - 1)) + h)) & 1
            shift = rows[tile, pl.ds(h, 1), :]
            loss = rows[tile, pl.ds(2 + h, 1), :]
            positive = rows[tile, pl.ds(4 + h, 1), :].astype(jnp.int32)
            mine = (positive >> 7) == slot
            shift = jnp.where(jnp.logical_or(mine, hit > 0), shift, DEAD)
            target = jnp.where(mine, positive & 127, -1)
            at = slice(side * QTILE, (side + 1) * QTILE)
            terms = jnp.exp2(scores[:, at] * factor + shift)
            terms = terms - jnp.where(column == target, loss, 0.0)
            halves.append(terms.astype(jnp.bfloat16))
        return jnp.concatenate(halves, axis=1)

    def next_scores(words):
        both = jnp.concatenate([q[tile_of(words[0])], q[tile_of(words[1])]], axis=0)
        return lax.dot_general(
            blocks[block_of(words[0])], both, (((1,), (1,)), ((), ())), preferred_element_type=jnp.float32
        )

    def step(i, coming):
        starting = tuple((items[2 * (UNROLL * i + u)], items[2 * (UNROLL * i + u) + 1]) for u in range(UNROLL))
        for u in range(UNROLL):
            grad = logit_grads(coming[u], scores[u])
            block_grads(coming[u], grad)
            scores[u] = next_scores(starting[u])
        return starting

    dead = jnp.int32(tiles)
    lax.fori_loop(0, counts[h] + 1, step, ((dead, dead),) * UNROLL)

    if last:
        summed.wait()

        def deliver(b, carry):
            block_acc[b] = (block_acc[b] + earlier[b]) * scale
            mate_acc[b] = ((block_acc[b + here] + earlier[b + here]) * scale).astype(jnp.bfloat16)
            return carry

        lax.fori_loop(0, here, deliver, 0, unroll=2)
        stores = [
            pltpu.make_async_copy(mate_acc, mate_out, sems.at[5]),
            pltpu.make_async_copy(block_acc.at[pl.ds(0, here)], own_out, sems.at[6]),
        ]
    else:
        stores = [pltpu.make_async_copy(block_acc, block_out, sems.at[5])]
    for store in stores:
        store.start()

    def finish(t, carry):
        query_grad[t] = (query_acc[t] * scale).T.astype(jnp.bfloat16)
        return carry

    part = tiles // 4
    for k in range(4):
        lax.fori_loop(k * part, (k + 1) * part, finish, 0, unroll=4)
        at = pl.ds(k * part, part)
        stores.append(pltpu.make_async_copy(query_grad.at[at], query_out.at[at], sems.at[8 + k]))
        stores[-1].start()
    for store in stores:
        store.wait()


def hold_kernel(kept, *rest):
    *lent, out = rest
    out[pl.ds(0, KEPT)] = kept[...]
    for k, part in enumerate(lent):
        out[pl.ds(KEPT + SLAB * k, SLAB)] = part[...]


def assemble_kernel(held, *rest):
    *back, out, built, sems = rest
    at = pl.ds(0, KEPT)
    kept = pltpu.make_async_copy(held.at[at], built.at[at], sems.at[0])
    kept.start()
    stores = []
    for k, part in enumerate(back):
        at = pl.ds(KEPT + SLAB * k, SLAB)
        built[at] = part[...].astype(jnp.float32)
        stores.append(pltpu.make_async_copy(built.at[at], out.at[at], sems.at[1 + k]))
        stores[-1].start()
    kept.wait()
    at = pl.ds(0, KEPT)
    stores.append(pltpu.make_async_copy(built.at[at], out.at[at], sems.at[1 + len(back)]))
    stores[-1].start()
    for store in stores:
        store.wait()


def shard_work(
    queries, index_rows, lse_shift, loss_weight, positives, tile_negs, fetch_owner, fetch_local
):
    narrow_count = lax.axis_size(NARROW)
    sources = lax.axis_size(SAME_CORE)
    core = lax.axis_index("c")
    narrow_pos = lax.axis_index(NARROW)
    feat_width = queries.shape[1]
    own_rows = queries.shape[0]
    blocks_here = index_rows.shape[0] // BLOCK
    stored = index_rows.reshape(blocks_here, BLOCK, feat_width)
    halves = []
    for h in range(2):
        part = queries[h * QTILE : (h + 1) * QTILE]
        spread = jnp.broadcast_to(part[None], (sources, QTILE, feat_width))
        halves.append(lax.all_to_all(spread, SAME_CORE, 0, 0, tiled=True))
    ring = lax.axis_size("x")
    ways = []
    for axis, shift in STEPS:
        size = lax.axis_size(axis)
        ways.append((axis, [(i, (i + shift) % size) for i in range(size)]))
    slabs = [slice(KEPT + SLAB * k, KEPT + SLAB * (k + 1)) for k in range(len(STEPS))]
    lent = [lax.ppermute(stored[at], axis, way) for at, (axis, way) in zip(slabs, ways)]
    kept = stored[:KEPT]
    smem = pl.BlockSpec(memory_space=pltpu.SMEM)
    vmem = pl.BlockSpec(memory_space=pltpu.VMEM)
    hbm = pl.BlockSpec(memory_space=pltpu.HBM)
    limit = pltpu.CompilerParams(vmem_limit_bytes=VMEM_LIMIT)
    owners = fetch_owner[:, 0]
    fetch_count = owners.shape[0]
    first_slot = narrow_pos * fetch_count
    slot_ids = first_slot + jnp.arange(fetch_count, dtype=jnp.int32)
    tile_hit = jnp.any(tile_negs[:, :, None] == slot_ids[None, None, :], axis=1)
    tiles = tile_negs.shape[0]
    pos_slots = positives.reshape(tiles, QTILE) // BLOCK
    pos_hit = jnp.any(pos_slots[:, :, None] == slot_ids[None, None, :], axis=1)
    ask = pl.pallas_call(
        functools.partial(ask_kernel, (ring, narrow_count, blocks_here)),
        out_shape=jax.ShapeDtypeStruct((sources, 2 * QTILE), jnp.int32),
        in_specs=[smem] * 5,
        out_specs=smem,
        cost_estimate=pl.CostEstimate(flops=10**6, bytes_accessed=2**16, transcendentals=0),
        name="ask",
    )
    hits = tile_bits(tile_hit)
    lives = tile_bits(jnp.logical_or(tile_hit, pos_hit))
    table = ask(jnp.stack([first_slot, core]), owners, fetch_local, hits, lives)
    first_row = narrow_pos * own_rows
    lse_own = lax.dynamic_slice_in_dim(lse_shift, first_row, own_rows, 0)
    loss_own = lax.dynamic_slice_in_dim(loss_weight, first_row, own_rows, 0)
    pos_own = lax.dynamic_slice_in_dim(positives, first_row, own_rows, 0)
    lse_full = lse_own + math.log(fetch_count * narrow_count * BLOCK)
    shift = jnp.log2(loss_own) - lse_full * math.log2(math.e)
    per_query = jnp.concatenate([shift, loss_own, pos_own.astype(jnp.float32)]).reshape(6, QTILE)
    per_query = jnp.broadcast_to(per_query[None], (sources, 6, QTILE))
    packed = table.astype(jnp.float32).reshape(sources, 2, QTILE)
    packed = jnp.concatenate([per_query, packed], axis=1)
    rows = lax.all_to_all(packed, SAME_CORE, 0, 0, tiled=True)
    table = rows[:, 6:].astype(jnp.int32).reshape(sources, 2 * QTILE)
    most = -(-(sources * PLACES * (tiles // 2) + 4 * UNROLL) // PIECE) * PIECE
    list_shape = jax.ShapeDtypeStruct((most,), jnp.int32)
    entry_shape = jax.ShapeDtypeStruct((sources * PLACES,), jnp.int32)
    listing = pl.pallas_call(
        list_kernel,
        out_shape=(list_shape, list_shape, jax.ShapeDtypeStruct((2,), jnp.int32), entry_shape, entry_shape),
        in_specs=[smem],
        out_specs=(hbm, hbm) + (smem,) * 3,
        scratch_shapes=[
            pltpu.SMEM(entry_shape.shape, jnp.int32),
            pltpu.SMEM((most,), jnp.int32),
            pltpu.SMEM((most,), jnp.int32),
            pltpu.SemaphoreType.DMA((2,)),
        ],
        cost_estimate=pl.CostEstimate(flops=10**9, bytes_accessed=2**20, transcendentals=0),
        name="listing",
    )
    *items, counts, base, hits = listing(table)
    hold = pl.pallas_call(
        hold_kernel,
        out_shape=jax.ShapeDtypeStruct(stored.shape, stored.dtype),
        in_specs=[vmem] * (1 + len(lent)),
        out_specs=vmem,
        compiler_params=limit,
        cost_estimate=pl.CostEstimate(flops=10**6, bytes_accessed=2**22, transcendentals=0),
        name="hold",
    )
    held = hold(kept, *lent)
    mate_held = lax.ppermute(held, "c", [(0, 1), (1, 0)])

    acc_shape = jax.ShapeDtypeStruct((2 * blocks_here, BLOCK, feat_width), jnp.float32)
    grad_shape = jax.ShapeDtypeStruct((sources, QTILE, feat_width), jnp.bfloat16)
    own_shape = jax.ShapeDtypeStruct((blocks_here, BLOCK, feat_width), jnp.float32)
    mate_shape = jax.ShapeDtypeStruct((blocks_here, BLOCK, feat_width), jnp.bfloat16)

    def scratch(extra):
        return extra + [
            pltpu.SMEM((most,), jnp.int32),
            pltpu.VMEM((sources + 1, 8, QTILE), jnp.float32),
            pltpu.VMEM((sources + 1, QTILE, feat_width), jnp.bfloat16),
            pltpu.VMEM((2 * blocks_here, BLOCK, feat_width), jnp.bfloat16),
            pltpu.VMEM((sources + 1, feat_width, QTILE), jnp.float32),
            pltpu.VMEM(acc_shape.shape, jnp.float32),
            pltpu.VMEM((UNROLL, BLOCK, 2 * QTILE), jnp.float32),
            pltpu.VMEM(grad_shape.shape, jnp.bfloat16),
            pltpu.SemaphoreType.DMA((12,)),
        ]

    cost = pl.CostEstimate(flops=2 * 10**10, bytes_accessed=2**25, transcendentals=10**7)
    chunk_0 = pl.pallas_call(
        functools.partial(chunk_kernel, 0, False),
        out_shape=(grad_shape, acc_shape),
        in_specs=[smem] * 3 + [hbm] * 5,
        out_specs=(hbm, hbm),
        scratch_shapes=scratch([]),
        compiler_params=limit,
        cost_estimate=cost,
        name="chunk_0",
    )
    grad_0, acc = chunk_0(counts, base, hits, items[0], rows, halves[0], held, mate_held)
    chunk_1 = pl.pallas_call(
        functools.partial(chunk_kernel, 1, True),
        out_shape=(grad_shape, own_shape, mate_shape),
        in_specs=[smem] * 3 + [hbm] * 6,
        out_specs=(hbm, hbm, hbm),
        scratch_shapes=scratch(
            [pltpu.VMEM(acc_shape.shape, jnp.float32), pltpu.VMEM(mate_shape.shape, jnp.bfloat16)]
        ),
        compiler_params=limit,
        cost_estimate=cost,
        name="chunk_1",
    )
    grad_1, own_grad, mate_grad = chunk_1(counts, base, hits, items[1], rows, halves[1], held, mate_held, acc)
    sums = []
    for part in (grad_0, grad_1):
        came = lax.all_to_all(part, SAME_CORE, 0, 0, tiled=True)
        sums.append(jnp.sum(came.astype(jnp.float32), axis=0))
    query_grad = jnp.concatenate(sums)
    from_mate = lax.ppermute(mate_grad, "c", [(0, 1), (1, 0)])
    held_grad = own_grad + from_mate.astype(jnp.float32)
    back = [
        lax.ppermute(held_grad[at].astype(jnp.bfloat16), axis, [(j, i) for i, j in way])
        for at, (axis, way) in zip(slabs, ways)
    ]
    assemble = pl.pallas_call(
        assemble_kernel,
        out_shape=own_shape,
        in_specs=[hbm] + [vmem] * len(back),
        out_specs=hbm,
        scratch_shapes=[
            pltpu.VMEM(own_shape.shape, jnp.float32),
            pltpu.SemaphoreType.DMA((2 + len(back),)),
        ],
        compiler_params=limit,
        cost_estimate=pl.CostEstimate(flops=10**6, bytes_accessed=2**23, transcendentals=0),
        name="assemble",
    )
    index_grad = assemble(held_grad, *back)
    return (query_grad, index_grad.reshape(blocks_here * BLOCK, feat_width))


def solution(mesh):
    wide, narrow = mesh.devices.shape
    split = Mesh(mesh.devices.reshape(wide // 2, 2, 4, narrow // 4), ("y", "c", "z", "x"))
    every = ("y", "c", "z", "x")
    group = ("y", "c")
    in_specs = (
        P(every, None),
        P(every, None),
        P(group),
        P(group),
        P(group),
        P(group, None),
        P(every, None),
        P(every),
    )
    out_specs = (P(every, None), P(every, None))
    return jax.shard_map(shard_work, mesh=split, in_specs=in_specs, out_specs=out_specs, check_vma=False)
```

```python
import functools
import math

import jax
import jax.numpy as jnp
from jax import lax
from jax.experimental import pallas as pl
from jax.experimental.pallas import tpu as pltpu
from jax.sharding import Mesh
from jax.sharding import PartitionSpec as P


BLOCK = 128
QTILE = 128
CAP = 2
SAME_CORE = ("y", "z", "x")
NARROW = ("z", "x")
KEPT = 16
SLAB = 8
STEPS = (("x", 1), ("x", -1), ("y", 1), ("y", -1), ("z", 1), ("z", -1))
PLACES = 2 * CAP * (1 + len(STEPS))
FIELDS = 6
COUNT_AT = PLACES * FIELDS
DEAD = -1e30
UNROLL = 12
PIECE = 2048
VMEM_LIMIT = 60 * 1024 * 1024


def tile_bits(flags):
    places = jnp.arange(flags.shape[0], dtype=jnp.int32)[:, None]
    return jnp.sum(jnp.left_shift(flags.astype(jnp.int32), places), axis=0)


def ask_kernel(sizes, where, owner, local, hits, lives, table):
    ring, narrow_count, blocks_here = sizes
    ring_bits, narrow_bits = ring.bit_length() - 1, narrow_count.bit_length() - 1
    slab_bits = SLAB.bit_length() - 1
    first_slot, core = where[0], where[1]

    def clear(d, carry):
        table[d, COUNT_AT] = 0
        return carry

    lax.fori_loop(0, table.shape[0], clear, 0, unroll=8)

    def ask(j, carry):
        own, block = owner[j], local[j]
        wide = own >> narrow_bits
        narrow = own & (narrow_count - 1)
        turn = (block - KEPT) >> slab_bits
        spot = {"y": wide >> 1, "z": narrow >> ring_bits, "x": narrow & (ring - 1)}
        for k, (axis, shift) in enumerate(STEPS):
            spot[axis] = spot[axis] + jnp.where(turn == k, shift + ring, 0)
        edge = ring - 1
        dest = ((spot["y"] & edge) << (2 * ring_bits)) | ((spot["z"] & edge) << ring_bits) | (spot["x"] & edge)
        place = table[dest, COUNT_AT]
        table[dest, COUNT_AT] = place + 1
        at = place * FIELDS
        table[dest, at] = jnp.where((wide & 1) == core, 0, blocks_here) + block
        table[dest, at + 1] = first_slot + j
        table[dest, at + 2] = hits[j] & 0xFFFF
        table[dest, at + 3] = (hits[j] >> 16) & 0xFFFF
        table[dest, at + 4] = lives[j] & 0xFFFF
        table[dest, at + 5] = (lives[j] >> 16) & 0xFFFF
        return carry

    lax.fori_loop(0, owner.shape[0], ask, 0, unroll=4)


def list_kernel(table, first_out, second_out, counts, base, hits, live, first_items, second_items, sems):
    groups = 4
    sources = table.shape[0]
    in_group = sources // groups
    dead = jnp.int32(sources)
    lists = (first_items, second_items)

    def group_entries(group, cursor):
        begin = cursor[2]

        def source_entries(n, count):
            src = group * in_group + n

            def place_entry(place, count):
                at = place * FIELDS
                base[count] = table[src, at] | (table[src, at + 1] << 7)
                hits[count] = table[src, at + 2] | (table[src, at + 3] << 16)
                live[count] = table[src, at + 4] | (table[src, at + 5] << 16)
                return count + 1

            return lax.fori_loop(0, table[src, COUNT_AT], place_entry, count)

        finish = lax.fori_loop(0, in_group, source_entries, begin)

        def entry_items(e, ends):
            start = (e << 7) + group * in_group
            alive = live[e]
            empty = (e << 7) + dead
            out = []
            for h, at in enumerate(ends):
                for n in range(in_group):
                    lists[h][at] = start + n
                    at = at + ((alive >> (2 * n + h)) & 1)
                lists[h][at] = empty
                out.append(at + (at & 1))
            return tuple(out)

        ends = lax.fori_loop(begin, finish, entry_items, cursor[:2])
        return ends + (finish,)

    zero = jnp.int32(0)
    base[0] = zero
    hits[0] = zero
    ends = lax.fori_loop(0, groups, group_entries, (zero, zero, zero))
    for h in range(2):
        for i in range(4 * UNROLL):
            lists[h][ends[h] + i] = dead
        count = (ends[h] + 2 * UNROLL - 1) // (2 * UNROLL)
        counts[h] = count
        target = (first_out, second_out)[h]

        def store_items(i, carry, h=h, target=target):
            at = pl.ds(pl.multiple_of(i * PIECE, PIECE), PIECE)
            piece = pltpu.make_async_copy(lists[h].at[at], target.at[at], sems.at[h])
            piece.start()
            piece.wait()
            return carry

        lax.fori_loop(0, (2 * UNROLL * (count + 1) + PIECE - 1) // PIECE, store_items, 0)


def chunk_kernel(h, last, counts, base, hits, items_in, rows_in, q_in, own_in, mate_in, *rest):
    if last:
        earlier_in, query_out, own_out, mate_out, earlier, mate_acc = rest[:6]
    else:
        query_out, block_out = rest[:2]
    items, rows, q, blocks, query_acc, block_acc, scores, query_grad, sems = rest[-9:]
    scale = 2.0 / math.sqrt(q.shape[2])
    factor = scale * math.log2(math.e)
    tiles = q_in.shape[0]
    here = own_in.shape[0]
    loads = [
        pltpu.make_async_copy(q_in, q.at[pl.ds(0, tiles)], sems.at[0]),
        pltpu.make_async_copy(own_in, blocks.at[pl.ds(0, here)], sems.at[1]),
        pltpu.make_async_copy(mate_in, blocks.at[pl.ds(here, here)], sems.at[2]),
        pltpu.make_async_copy(rows_in, rows.at[pl.ds(0, tiles)], sems.at[3]),
    ]
    if last:
        summed = pltpu.make_async_copy(earlier_in, earlier, sems.at[4])
    for load in loads:
        load.start()
    if last:
        summed.start()

    def load_items(i, carry):
        at = pl.ds(pl.multiple_of(i * PIECE, PIECE), PIECE)
        piece = pltpu.make_async_copy(items_in.at[at], items.at[at], sems.at[7])
        piece.start()
        piece.wait()
        return carry

    lax.fori_loop(0, (2 * UNROLL * (counts[h] + 1) + PIECE - 1) // PIECE, load_items, 0)
    zero = jnp.zeros((BLOCK, QTILE), jnp.float32)
    q[tiles] = zero.astype(q.dtype)
    rows[tiles] = jnp.full(rows.shape[1:], -1.0, jnp.float32)
    query_acc[tiles] = zero

    def clear_query(t, carry):
        query_acc[t] = zero
        return carry

    def clear_block(b, carry):
        block_acc[b] = zero
        return carry

    lax.fori_loop(0, tiles, clear_query, 0, unroll=4)
    lax.fori_loop(0, 2 * here, clear_block, 0, unroll=4)
    scores[...] = jnp.zeros_like(scores)
    for load in loads:
        load.wait()

    column = lax.broadcasted_iota(jnp.int32, (BLOCK, QTILE), 0)

    def tile_of(word):
        return word & 127

    def block_of(word):
        return base[word >> 7] & 127

    def block_grads(words, grad):
        block = block_of(words[0])
        t1, t2 = tile_of(words[0]), tile_of(words[1])
        both = jnp.concatenate([q[t1], q[t2]], axis=0)
        to_block = jnp.dot(grad, both, preferred_element_type=jnp.float32)
        part = lax.dot_general(
            blocks[block], grad, (((0,), (0,)), ((), ())), preferred_element_type=jnp.float32
        )
        block_acc[block] += to_block
        sum1 = query_acc[t1] + part[:, :QTILE]
        sum2 = query_acc[t2] + part[:, QTILE:]
        query_acc[t1] = sum1
        query_acc[t2] = sum2

    def logit_grads(words, scores):
        slot = base[words[0] >> 7] >> 7
        halves = []
        for side, word in enumerate(words):
            tile = tile_of(word)
            hit = (hits[word >> 7] >> (2 * (tile & (tiles // 4 - 1)) + h)) & 1
            shift = rows[tile, pl.ds(h, 1), :]
            loss = rows[tile, pl.ds(2 + h, 1), :]
            positive = rows[tile, pl.ds(4 + h, 1), :].astype(jnp.int32)
            mine = (positive >> 7) == slot
            shift = jnp.where(jnp.logical_or(mine, hit > 0), shift, DEAD)
            target = jnp.where(mine, positive & 127, -1)
            at = slice(side * QTILE, (side + 1) * QTILE)
            terms = jnp.exp2(scores[:, at] * factor + shift)
            terms = terms - jnp.where(column == target, loss, 0.0)
            halves.append(terms.astype(jnp.bfloat16))
        return jnp.concatenate(halves, axis=1)

    def next_scores(words):
        both = jnp.concatenate([q[tile_of(words[0])], q[tile_of(words[1])]], axis=0)
        return lax.dot_general(
            blocks[block_of(words[0])], both, (((1,), (1,)), ((), ())), preferred_element_type=jnp.float32
        )

    def step(i, coming):
        starting = tuple((items[2 * (UNROLL * i + u)], items[2 * (UNROLL * i + u) + 1]) for u in range(UNROLL))
        for u in range(UNROLL):
            grad = logit_grads(coming[u], scores[u])
            block_grads(coming[u], grad)
            scores[u] = next_scores(starting[u])
        return starting

    dead = jnp.int32(tiles)
    lax.fori_loop(0, counts[h] + 1, step, ((dead, dead),) * UNROLL)

    if last:
        summed.wait()

        def deliver(b, carry):
            block_acc[b] = (block_acc[b] + earlier[b]) * scale
            mate_acc[b] = ((block_acc[b + here] + earlier[b + here]) * scale).astype(jnp.bfloat16)
            return carry

        lax.fori_loop(0, here, deliver, 0, unroll=2)
        stores = [
            pltpu.make_async_copy(mate_acc, mate_out, sems.at[5]),
            pltpu.make_async_copy(block_acc.at[pl.ds(0, here)], own_out, sems.at[6]),
        ]
    else:
        stores = [pltpu.make_async_copy(block_acc, block_out, sems.at[5])]
    for store in stores:
        store.start()

    def finish(t, carry):
        query_grad[t] = (query_acc[t] * scale).T.astype(jnp.bfloat16)
        return carry

    part = tiles // 4
    for k in range(4):
        lax.fori_loop(k * part, (k + 1) * part, finish, 0, unroll=4)
        at = pl.ds(k * part, part)
        stores.append(pltpu.make_async_copy(query_grad.at[at], query_out.at[at], sems.at[8 + k]))
        stores[-1].start()
    for store in stores:
        store.wait()


def hold_kernel(kept, *rest):
    *lent, out = rest
    out[pl.ds(0, KEPT)] = kept[...]
    for k, part in enumerate(lent):
        out[pl.ds(KEPT + SLAB * k, SLAB)] = part[...]


def assemble_kernel(kept, *rest):
    *back, out = rest
    out[pl.ds(0, KEPT)] = kept[...]
    for k, part in enumerate(back):
        out[pl.ds(KEPT + SLAB * k, SLAB)] = part[...].astype(jnp.float32)


def shard_work(
    queries, index_rows, lse_shift, loss_weight, positives, tile_negs, fetch_owner, fetch_local
):
    narrow_count = lax.axis_size(NARROW)
    sources = lax.axis_size(SAME_CORE)
    core = lax.axis_index("c")
    narrow_pos = lax.axis_index(NARROW)
    feat_width = queries.shape[1]
    own_rows = queries.shape[0]
    blocks_here = index_rows.shape[0] // BLOCK
    stored = index_rows.reshape(blocks_here, BLOCK, feat_width)
    halves = []
    for h in range(2):
        part = queries[h * QTILE : (h + 1) * QTILE]
        spread = jnp.broadcast_to(part[None], (sources, QTILE, feat_width))
        halves.append(lax.all_to_all(spread, SAME_CORE, 0, 0, tiled=True))
    ring = lax.axis_size("x")
    ways = []
    for axis, shift in STEPS:
        size = lax.axis_size(axis)
        ways.append((axis, [(i, (i + shift) % size) for i in range(size)]))
    slabs = [slice(KEPT + SLAB * k, KEPT + SLAB * (k + 1)) for k in range(len(STEPS))]
    lent = [lax.ppermute(stored[at], axis, way) for at, (axis, way) in zip(slabs, ways)]
    kept = stored[:KEPT]
    smem = pl.BlockSpec(memory_space=pltpu.SMEM)
    vmem = pl.BlockSpec(memory_space=pltpu.VMEM)
    hbm = pl.BlockSpec(memory_space=pltpu.HBM)
    limit = pltpu.CompilerParams(vmem_limit_bytes=VMEM_LIMIT)
    owners = fetch_owner[:, 0]
    fetch_count = owners.shape[0]
    first_slot = narrow_pos * fetch_count
    slot_ids = first_slot + jnp.arange(fetch_count, dtype=jnp.int32)
    tile_hit = jnp.any(tile_negs[:, :, None] == slot_ids[None, None, :], axis=1)
    tiles = tile_negs.shape[0]
    pos_slots = positives.reshape(tiles, QTILE) // BLOCK
    pos_hit = jnp.any(pos_slots[:, :, None] == slot_ids[None, None, :], axis=1)
    ask = pl.pallas_call(
        functools.partial(ask_kernel, (ring, narrow_count, blocks_here)),
        out_shape=jax.ShapeDtypeStruct((sources, 2 * QTILE), jnp.int32),
        in_specs=[smem] * 5,
        out_specs=smem,
        cost_estimate=pl.CostEstimate(flops=10**6, bytes_accessed=2**16, transcendentals=0),
        name="ask",
    )
    hits = tile_bits(tile_hit)
    lives = tile_bits(jnp.logical_or(tile_hit, pos_hit))
    table = ask(jnp.stack([first_slot, core]), owners, fetch_local, hits, lives)
    first_row = narrow_pos * own_rows
    lse_own = lax.dynamic_slice_in_dim(lse_shift, first_row, own_rows, 0)
    loss_own = lax.dynamic_slice_in_dim(loss_weight, first_row, own_rows, 0)
    pos_own = lax.dynamic_slice_in_dim(positives, first_row, own_rows, 0)
    lse_full = lse_own + math.log(fetch_count * narrow_count * BLOCK)
    shift = jnp.log2(loss_own) - lse_full * math.log2(math.e)
    per_query = jnp.concatenate([shift, loss_own, pos_own.astype(jnp.float32)]).reshape(6, QTILE)
    per_query = jnp.broadcast_to(per_query[None], (sources, 6, QTILE))
    packed = table.astype(jnp.float32).reshape(sources, 2, QTILE)
    packed = jnp.concatenate([per_query, packed], axis=1)
    rows = lax.all_to_all(packed, SAME_CORE, 0, 0, tiled=True)
    table = rows[:, 6:].astype(jnp.int32).reshape(sources, 2 * QTILE)
    most = -(-(sources * PLACES * (tiles // 2) + 4 * UNROLL) // PIECE) * PIECE
    list_shape = jax.ShapeDtypeStruct((most,), jnp.int32)
    entry_shape = jax.ShapeDtypeStruct((sources * PLACES,), jnp.int32)
    listing = pl.pallas_call(
        list_kernel,
        out_shape=(list_shape, list_shape, jax.ShapeDtypeStruct((2,), jnp.int32), entry_shape, entry_shape),
        in_specs=[smem],
        out_specs=(hbm, hbm) + (smem,) * 3,
        scratch_shapes=[
            pltpu.SMEM(entry_shape.shape, jnp.int32),
            pltpu.SMEM((most,), jnp.int32),
            pltpu.SMEM((most,), jnp.int32),
            pltpu.SemaphoreType.DMA((2,)),
        ],
        cost_estimate=pl.CostEstimate(flops=10**9, bytes_accessed=2**20, transcendentals=0),
        name="listing",
    )
    *items, counts, base, hits = listing(table)
    hold = pl.pallas_call(
        hold_kernel,
        out_shape=jax.ShapeDtypeStruct(stored.shape, stored.dtype),
        in_specs=[vmem] * (1 + len(lent)),
        out_specs=vmem,
        compiler_params=limit,
        cost_estimate=pl.CostEstimate(flops=10**6, bytes_accessed=2**22, transcendentals=0),
        name="hold",
    )
    held = hold(kept, *lent)
    mate_held = lax.ppermute(held, "c", [(0, 1), (1, 0)])

    acc_shape = jax.ShapeDtypeStruct((2 * blocks_here, BLOCK, feat_width), jnp.float32)
    grad_shape = jax.ShapeDtypeStruct((sources, QTILE, feat_width), jnp.bfloat16)
    own_shape = jax.ShapeDtypeStruct((blocks_here, BLOCK, feat_width), jnp.float32)
    mate_shape = jax.ShapeDtypeStruct((blocks_here, BLOCK, feat_width), jnp.bfloat16)

    def scratch(extra):
        return extra + [
            pltpu.SMEM((most,), jnp.int32),
            pltpu.VMEM((sources + 1, 8, QTILE), jnp.float32),
            pltpu.VMEM((sources + 1, QTILE, feat_width), jnp.bfloat16),
            pltpu.VMEM((2 * blocks_here, BLOCK, feat_width), jnp.bfloat16),
            pltpu.VMEM((sources + 1, feat_width, QTILE), jnp.float32),
            pltpu.VMEM(acc_shape.shape, jnp.float32),
            pltpu.VMEM((UNROLL, BLOCK, 2 * QTILE), jnp.float32),
            pltpu.VMEM(grad_shape.shape, jnp.bfloat16),
            pltpu.SemaphoreType.DMA((12,)),
        ]

    cost = pl.CostEstimate(flops=2 * 10**10, bytes_accessed=2**25, transcendentals=10**7)
    chunk_0 = pl.pallas_call(
        functools.partial(chunk_kernel, 0, False),
        out_shape=(grad_shape, acc_shape),
        in_specs=[smem] * 3 + [hbm] * 5,
        out_specs=(hbm, hbm),
        scratch_shapes=scratch([]),
        compiler_params=limit,
        cost_estimate=cost,
        name="chunk_0",
    )
    grad_0, acc = chunk_0(counts, base, hits, items[0], rows, halves[0], held, mate_held)
    chunk_1 = pl.pallas_call(
        functools.partial(chunk_kernel, 1, True),
        out_shape=(grad_shape, own_shape, mate_shape),
        in_specs=[smem] * 3 + [hbm] * 6,
        out_specs=(hbm, hbm, hbm),
        scratch_shapes=scratch(
            [pltpu.VMEM(acc_shape.shape, jnp.float32), pltpu.VMEM(mate_shape.shape, jnp.bfloat16)]
        ),
        compiler_params=limit,
        cost_estimate=cost,
        name="chunk_1",
    )
    grad_1, own_grad, mate_grad = chunk_1(counts, base, hits, items[1], rows, halves[1], held, mate_held, acc)
    sums = []
    for part in (grad_0, grad_1):
        came = lax.all_to_all(part, SAME_CORE, 0, 0, tiled=True)
        sums.append(jnp.sum(came.astype(jnp.float32), axis=0))
    query_grad = jnp.concatenate(sums)
    from_mate = lax.ppermute(mate_grad, "c", [(0, 1), (1, 0)])
    held_grad = own_grad + from_mate.astype(jnp.float32)
    back = [
        lax.ppermute(held_grad[at].astype(jnp.bfloat16), axis, [(j, i) for i, j in way])
        for at, (axis, way) in zip(slabs, ways)
    ]
    assemble = pl.pallas_call(
        assemble_kernel,
        out_shape=own_shape,
        in_specs=[vmem] * (1 + len(back)),
        out_specs=vmem,
        compiler_params=limit,
        cost_estimate=pl.CostEstimate(flops=10**6, bytes_accessed=2**23, transcendentals=0),
        name="assemble",
    )
    index_grad = assemble(held_grad[:KEPT], *back)
    return (query_grad, index_grad.reshape(blocks_here * BLOCK, feat_width))


def solution(mesh):
    wide, narrow = mesh.devices.shape
    split = Mesh(mesh.devices.reshape(wide // 2, 2, 4, narrow // 4), ("y", "c", "z", "x"))
    every = ("y", "c", "z", "x")
    group = ("y", "c")
    in_specs = (
        P(every, None),
        P(every, None),
        P(group),
        P(group),
        P(group),
        P(group, None),
        P(every, None),
        P(every),
    )
    out_specs = (P(every, None), P(every, None))
    return jax.shard_map(shard_work, mesh=split, in_specs=in_specs, out_specs=out_specs, check_vma=False)
```
